256 devices in a mesh: wide: 32 (over z, y), narrow: 8 (over x, core).
Axes of the slice: x: 4, y: 4, z: 8, core: 2. Of those that a mesh axis runs over, the one named last changes fastest.
Arguments:
- hidden: bfloat16 [160, 4096], P('wide', 'narrow'), may hold values from -18 to 18
- w_query: bfloat16 [4096, 4096], P('narrow', 'wide'), may hold values from -0.09375 to 0.09375
- w_keyval: bfloat16 [4096, 1024], P('narrow', 'wide'), may hold values from -0.09375 to 0.09375
- w_out: bfloat16 [4096, 4096], P('narrow', 'wide'), may hold values from -0.09375 to 0.09375
- pool: bfloat16 [16384, 16, 1024], P(('wide', 'narrow')), may hold values from -144 to 144
- page_req: int32 [16384], P(('wide', 'narrow')), may hold values from -1 to 31, as said below
- page_idx: int32 [16384], P(('wide', 'narrow')), may hold values from -1 to 511, as said below
- lengths: int32 [32], replicated, may hold values from 128 to 8192, as said below
- moves: int32 [16384, 1], P(('wide', 'narrow')), may hold values from 0 to 31; in each aligned block of 64 rows (0 to 63, 64 to 127, ...) at most 2 rows name the same one
- accepted: int32 [32], replicated, may hold values from 1 to 5
Outputs:
- attended: bfloat16 [160, 4096], P('narrow', 'wide')
- new_entries: bfloat16 [32, 5, 1024], P('wide')
- moved_pool: bfloat16 [16384, 16, 1024], P(('wide', 'narrow'))
- moved_req: int32 [16384], P(('wide', 'narrow'))
- moved_idx: int32 [16384], P(('wide', 'narrow'))
The draws below stay inside these ranges and needn't reach their ends.
Inputs may be any that keep to these rules, and one draw needn't show every extreme that they name: Request r holds exactly ceil(lengths[r] / 16) slots, whose page numbers are 0 up to that count minus 1, each once; every other slot is free, with page_req and page_idx -1. `page_idx`: see page_req. `lengths`: each length lies either in 128 to 256 or in 6144 to 8192; exactly 16 lie in the second range. `moves`: each device sends exactly 2 of its slots to each index of wide.
All inputs are finite; a program needn't handle non-finite values.
Results may differ from the reference program's by a relative error of at most 0.03.
Values may be sent and summed in bfloat16 or wider, within the bound.
A program may use at most 128 MiB of HBM per device.

```python
import math
import jax
import jax.numpy as jnp
import numpy as np
from jax import lax

D = 4096
HEADS = 32
KVH = 4
HD = 128
KVW = 1024
STEPS = 5
PAGE = 16
MAXP = 512
REQ = 32
ROWS = 160
SLOTS = 16384
POOL = 64
CAP = 2
N_WIDE = 32
N_NARROW = 8


def request_lengths(key):
    first, second, third = jax.random.split(jax.random.fold_in(key, 11), 3)
    shuffled = jax.random.permutation(first, REQ)
    longflag = shuffled < REQ // 2
    long_len = jax.random.randint(second, (REQ,), 3 * MAXP * PAGE // 4, MAXP * PAGE + 1)
    short_len = jax.random.randint(third, (REQ,), 8 * PAGE, 16 * PAGE + 1)
    result = jnp.where(longflag, long_len, short_len)
    inverse = jnp.argsort(shuffled, stable=True)
    result = result.at[inverse[0]].set(MAXP * PAGE)
    result = result.at[inverse[REQ - 1]].set(8 * PAGE)
    return result.astype(jnp.int32)


def page_layout(key):
    slot_ids = jax.random.permutation(jax.random.fold_in(key, 7), SLOTS)
    owners = slot_ids // MAXP
    numbers = slot_ids % MAXP
    pages_held = (request_lengths(key) + PAGE - 1) // PAGE
    live_mask = numbers < jnp.take(pages_held, owners)
    return (jnp.where(live_mask, owners, -1), jnp.where(live_mask, numbers, -1))


def draw_lengths(key, part):
    return request_lengths(key)


def draw_page_req(key, part):
    return page_layout(key)[0].astype(jnp.int32)


def draw_page_idx(key, part):
    return page_layout(key)[1].astype(jnp.int32)


def draw_hidden(key, part):
    values = jnp.clip(jax.random.normal(jax.random.fold_in(key, 3), (ROWS, D), jnp.float32), -6.0, 6.0)
    return values.astype(jnp.bfloat16)


def draw_pool(key, part):
    values = jnp.clip(jax.random.normal(jax.random.fold_in(key, 13), (SLOTS, PAGE, KVW), jnp.float32), -6.0, 6.0)
    return values.astype(jnp.bfloat16)


def place_ends(array, key, least, top_value):
    longest = array.shape.index(max(array.shape))
    spots = []
    for shift in (0, 1):
        where = [jax.random.randint(jax.random.fold_in(key, axis), (), 0, length) for axis, length in enumerate(array.shape)]
        where[longest] = (where[longest] + shift) % array.shape[longest]
        spots.append(tuple(where))
    return array.at[spots[0]].set(least).at[spots[1]].set(top_value)


def steps_of(key, shape, cuts, smallest, top_value):
    loudness = 1.0
    for position, shards_of in cuts:
        heights = jax.random.uniform(jax.random.fold_in(jax.random.fold_in(key, 6), position), (shards_of,), jnp.float32, smallest / len(cuts), top_value / len(cuts))
        loudness = loudness * jnp.repeat(jnp.exp(heights), shape[position] // shards_of).reshape((-1,) + (1,) * (len(shape) - 1 - position))
    return loudness


def assign_block(own_key, own, number, rows, number_of, top, most, slope):
    order = jax.random.permutation(own_key, number_of)
    packed, usual = portions_of(number_of, rows * top, most, slope, True), portions_of(number_of, rows * top, most, slope, False)
    places = jnp.arange(number_of)

    def named(tallies, rotation):
        used = int((tallies > 0).sum())
        fixed = max(1, used // 4)
        shifted = fixed + (places - fixed + rotation * (used - fixed)) % max(1, number_of - fixed)
        return jnp.zeros((number_of,), jnp.int32).at[order[jnp.where(places < fixed, places, shifted)]].set(jnp.asarray(tallies, jnp.int32))

    tallies = jnp.where(number % 4 == 0, named(packed, number // 4), named(usual, number - number // 4 - 1))
    mixed = jax.random.permutation(jax.random.fold_in(own, 3), number_of)
    giver, taker = mixed[0:number_of // 2 * 2:2], mixed[1:number_of // 2 * 2:2]
    slack = jnp.minimum(tallies[giver] - 1, most - tallies[taker]) // 2
    slack = jnp.where((giver == order[0]) | (taker == order[0]) | (tallies[taker] == 0), 0, jnp.maximum(slack, 0))
    shifted = jax.random.randint(jax.random.fold_in(own, 4), (number_of // 2,), 0, 1 << 20) % (slack + 1)
    tallies = tallies.at[giver].add(-shifted).at[taker].add(shifted)
    items = jnp.searchsorted(jnp.cumsum(tallies), jnp.arange(rows * top), side="right").astype(jnp.int32)
    table = items.reshape(top, rows).T
    table = table[jax.random.permutation(jax.random.fold_in(own, 1), rows)]
    rotation = jax.random.randint(jax.random.fold_in(own, 2), (rows, 1), 0, top)
    return jnp.take_along_axis(table, (jnp.arange(top)[None, :] + rotation) % top, axis=1)


def portions_of(count, total, limit, lean, full):
    weights = [(1 << 20) // math.isqrt(grade ** lean) + 1 for grade in range(1, count + 1)]
    largest = limit if full else min(limit, max(-(-total // count), total * weights[0] // sum(weights)))
    least = 1 if total - largest >= count - 1 else 0
    given, rest = [largest] + [least] * (count - 1), total - largest - least * (count - 1)
    while rest > 0:
        free = [i for i in range(1, count) if given[i] < largest] or [i for i in range(1, count) if given[i] < limit]
        whole, budget = sum([weights[i] for i in free]), rest
        for i in free:
            extra = min(limit - given[i], max(1, budget * weights[i] // whole), rest)
            given[i] = given[i] + extra
            rest = rest - extra
    return np.array(given)


def bell_draw(own_key, dims, width, limit, pieces=(), kind=jnp.bfloat16):
    values = jax.random.normal(own_key, dims, jnp.float32) * width
    if len(pieces) > 0:
        values = steps_of(own_key, dims, pieces, -0.22, 0.18) * values
    return jnp.clip(values, min=-limit, max=limit).astype(kind)


def setup_inputs(seed: int = 0) -> dict:
    splits = jax.random.split(jax.random.key(seed), 11)
    hidden = draw_hidden(jax.random.fold_in(splits[10], 71), 0)
    w_query = bell_draw(splits[1], (D, D), D ** -0.5, 0.09375, ((0, 8), (1, 32)))
    w_keyval = bell_draw(splits[2], (D, KVW), D ** -0.5, 0.09375, ((0, 8), (1, 32)))
    w_out = bell_draw(splits[3], (D, D), D ** -0.5, 0.09375, ((0, 8), (1, 32)))
    pool = draw_pool(jax.random.fold_in(splits[10], 71), 0)
    page_req = draw_page_req(jax.random.fold_in(splits[10], 71), 0)
    page_idx = draw_page_idx(jax.random.fold_in(splits[10], 71), 0)
    lengths = draw_lengths(jax.random.fold_in(splits[10], 71), 0)
    moves_keys = jax.random.split(jax.random.fold_in(splits[8], 1), SLOTS // POOL)
    moves_turns = jax.random.permutation(jax.random.fold_in(splits[8], 3), SLOTS // POOL)
    moves = jax.vmap(lambda own, number: assign_block(jax.random.fold_in(splits[8], 2), own, number, POOL, N_WIDE, 1, CAP, 0))(moves_keys, moves_turns).reshape((SLOTS, 1))
    accepted = place_ends(jax.random.randint(splits[9], (REQ,), 1, STEPS + 1), jax.random.fold_in(splits[9], 1), 1, STEPS).astype(jnp.int32)
    return {"hidden": hidden, "w_query": w_query, "w_keyval": w_keyval, "w_out": w_out, "pool": pool, "page_req": page_req, "page_idx": page_idx, "lengths": lengths, "moves": moves, "accepted": accepted}


NEG_FILL = -1e+30

def reference(hidden, w_query, w_keyval, w_out, pool, page_req, page_idx, lengths, moves, accepted):
    groups = HEADS // KVH
    scale = 1.0 / math.sqrt(HD)
    query = jnp.dot(hidden, w_query, preferred_element_type=jnp.float32).astype(jnp.bfloat16)
    keyval = jnp.dot(hidden, w_keyval, preferred_element_type=jnp.float32).astype(jnp.bfloat16)
    query_r = query.reshape(REQ, STEPS, KVH, groups, HD)
    keyval_r = keyval.reshape(REQ, STEPS, 2, KVH, HD)
    live_key = jnp.where(page_req >= 0, page_req * MAXP + page_idx, REQ * MAXP).astype(jnp.int32)
    slot_of = jnp.zeros((REQ * MAXP,), jnp.int32).at[live_key].set(jnp.arange(SLOTS, dtype=jnp.int32), mode='drop')
    causal = jnp.arange(STEPS)[None, :] <= jnp.arange(STEPS)[:, None]
    positions = jnp.arange(MAXP * PAGE, dtype=jnp.int32)

    def one_request(index):
        slots = lax.dynamic_slice_in_dim(slot_of, index * MAXP, MAXP)
        cache = pool[slots].reshape(MAXP * PAGE, 2, KVH, HD)
        fresh = lax.dynamic_index_in_dim(keyval_r, index, 0, False)
        keys = jnp.concatenate([cache[:, 0], fresh[:, 0]], axis=0).astype(jnp.float32)
        values = jnp.concatenate([cache[:, 1], fresh[:, 1]], axis=0).astype(jnp.float32)
        queries = lax.dynamic_index_in_dim(query_r, index, 0, False).astype(jnp.float32)
        length = lax.dynamic_index_in_dim(lengths, index, 0, False)
        cache_ok = jnp.broadcast_to(positions[None, :] < length, (STEPS, MAXP * PAGE))
        allowed = jnp.concatenate([cache_ok, causal], axis=1)
        scores = jnp.einsum('skgd,tkd->kgst', queries, keys) * scale
        scores = jnp.where(allowed, scores, NEG_FILL)
        top = lax.optimization_barrier(jnp.max(scores, axis=-1, keepdims=True))
        weights = jnp.where(allowed, jnp.exp(scores - top), 0.0)
        total = lax.optimization_barrier(jnp.sum(weights, axis=-1))
        rounded = lax.optimization_barrier(weights.astype(jnp.bfloat16)).astype(jnp.float32)
        mixed = jnp.einsum('kgst,tkd->skgd', rounded, values)
        mixed = mixed / jnp.transpose(total, (2, 0, 1))[..., None]
        return mixed.astype(jnp.bfloat16)
    attn = lax.map(one_request, jnp.arange(REQ, dtype=jnp.int32)).reshape(ROWS, HEADS * HD)
    attended = jnp.dot(attn, w_out, preferred_element_type=jnp.float32).astype(jnp.bfloat16)
    step_ids = jnp.arange(STEPS, dtype=jnp.int32)
    new_entries = jnp.where(step_ids[None, :, None] < accepted[:, None, None], keyval.reshape(REQ, STEPS, KVW), jnp.zeros((), keyval.dtype))
    blocks = SLOTS // POOL
    dest = moves[:, 0].reshape(blocks, POOL)
    order = jnp.arange(POOL, dtype=jnp.int32)
    earlier = order[None, :] < order[:, None]
    rank = lax.optimization_barrier(jnp.sum((dest[:, :, None] == dest[:, None, :]) & earlier[None], axis=2)).astype(jnp.int32)
    block_ids = jnp.arange(blocks, dtype=jnp.int32)
    source_wide = block_ids // N_NARROW
    narrow_ids = block_ids % N_NARROW
    target = ((dest * N_NARROW + narrow_ids[:, None]) * POOL + source_wide[:, None] * CAP + rank).reshape(SLOTS)
    moved_pool = jnp.zeros_like(pool).at[target].set(pool)
    moved_req = jnp.zeros_like(page_req).at[target].set(page_req)
    moved_idx = jnp.zeros_like(page_idx).at[target].set(page_idx)
    return (attended, new_entries, moved_pool, moved_req, moved_idx)
```

```python
import functools
import math

import jax
import jax.numpy as jnp
from jax import lax
from jax.experimental import pallas as pl
from jax.experimental.pallas import tpu as pltpu
from jax.sharding import PartitionSpec as P

HEADS = 32
KVH = 4
HD = 128
STEPS = 5
PAGE = 16
WIDE = 32
NARROW = 8
NY = 4
NZ = 8
POOL = 64
CHUNK = 16
SCALE = 1.0 / math.sqrt(HD)
LOG2E = 1.4426950408889634
NEG = -1e30
F32 = jnp.float32
BF16 = jnp.bfloat16
I32 = jnp.int32
MESH = pl.DeviceIdType.MESH
VMEM_SPEC = pl.BlockSpec(memory_space=pltpu.VMEM)
SMEM_SPEC = pl.BlockSpec(memory_space=pltpu.SMEM)
ANY_SPEC = pl.BlockSpec(memory_space=pl.ANY)


def sort_kernel(moves, req, idx, lens, pool, sorted_out, live_out, meta, count, sem):
    def clear(d, _):
        count[d] = 0
        return 0

    lax.fori_loop(0, WIDE, clear, 0)

    def place(p, state):
        live, free = state
        d = moves[p]
        k = count[d]
        count[d] = k + 1
        r = req[p]
        i = idx[p]
        pltpu.make_async_copy(pool.at[p], sorted_out.at[k, d], sem.at[0]).start()
        meta[0, 2 * d + k] = r
        meta[0, POOL + 2 * d + k] = i
        alive = r >= 0
        pos = jnp.where(alive, live, POOL - 1 - free)
        pltpu.make_async_copy(pool.at[p], live_out.at[pos], sem.at[1]).start()
        seen = jnp.clip(lens[jnp.maximum(r, 0)] - i * PAGE, 0, PAGE)
        meta[1, pos] = r
        meta[1, POOL + pos] = jnp.where(alive, seen, 0)
        step = jnp.where(alive, 1, 0)
        return live + step, free + 1 - step

    live, _ = lax.fori_loop(0, POOL, place, (jnp.int32(0), jnp.int32(0)))
    meta[2, 0] = live
    pltpu.make_async_copy(live_out, live_out, sem.at[0]).wait()
    pltpu.make_async_copy(live_out, live_out, sem.at[1]).wait()


def enter(w, n):
    barrier = pltpu.get_barrier_semaphore()

    def wide_signal(k, _):
        pl.semaphore_signal(
            barrier, inc=1, device_id=((w + k) % WIDE, n), device_id_type=MESH
        )
        return 0

    def narrow_signal(k, _):
        pl.semaphore_signal(
            barrier, inc=1, device_id=(w, (n + k) % NARROW), device_id_type=MESH
        )
        return 0

    lax.fori_loop(1, WIDE, wide_signal, 0)
    lax.fori_loop(1, NARROW, narrow_signal, 0)
    pl.semaphore_wait(barrier, WIDE + NARROW - 2)


def remote(src, dst, send, recv, device):
    return pltpu.make_async_remote_copy(
        src_ref=src,
        dst_ref=dst,
        send_sem=send,
        recv_sem=recv,
        device_id=device,
        device_id_type=MESH,
    )


def gather_kernel(
    hidden, w_query, w_kv_t, meta, leaving, pages,
    query_out, kvrow_out, kv_out, moved_out, meta_wide, meta_narrow,
    hid_own, hid_all, send_b, recv_b, q_own, kv_tiles, kv_parts, meta_w, meta_n,
    s_a, r_a, s_m, r_m, s_mn, r_mn, s_mig, r_mig, l_sem, s_x, r_x, s_p, r_p,
    s_b, r_b, s_c1, r_c1, s_k1, r_k1, s_c2, r_c2, s_k2, r_k2, s_c3, r_c3,
):
    w = lax.axis_index("wide")
    n = lax.axis_index("narrow")
    z = w // NY
    y = w % NY
    x = n // 2
    c = n % 2
    other = 2 * x + (1 - c)
    hub = n == z
    hid_own[...] = jnp.zeros_like(hid_own)
    hid_own[0:STEPS, :] = hidden[...]
    hid_all[pl.ds(w, 1)] = hid_own[...][None]
    meta_w[pl.ds(w, 1)] = meta[...][None]
    meta_n[pl.ds(n, 1)] = meta[...][None]
    enter(w, n)

    def send_hidden(k, _):
        remote(hid_own, hid_all.at[w], s_a, r_a, ((w + k) % WIDE, n)).start()
        return 0

    lax.fori_loop(1, WIDE, send_hidden, 0)

    def key_block(head):
        return pl.ds(pl.multiple_of(HD * head, HD), HD)

    def value_block(head):
        return pl.ds(pl.multiple_of(KVH * HD + HD * head, HD), HD)

    for dx in (1, 3, 2):
        tx = (x + dx) % 4
        for part, block in ((0, key_block(tx)), (1, value_block(tx))):
            remote(
                pages.at[:, :, block], kv_out.at[n, part], s_x, r_x.at[dx - 1], (w, 2 * tx + c)
            ).start()
    own_copies = []
    for part, block in ((0, key_block(x)), (1, value_block(x))):
        remote(pages.at[:, :, block], kv_out.at[n, part], s_p, r_p.at[0], (w, other)).start()
        own = pltpu.make_async_copy(pages.at[:, :, block], kv_out.at[n, part], l_sem.at[part])
        own.start()
        own_copies.append(own)

    def send_page(k, _):
        peer = (w + k) % WIDE
        remote(leaving.at[0, peer], moved_out.at[w], s_mig, r_mig, (peer, n)).start()
        return 0

    lax.fori_loop(1, WIDE, send_page, 0)
    stay = pltpu.make_async_copy(leaving.at[0, w], moved_out.at[w], l_sem.at[2])
    stay.start()

    def send_meta(k, _):
        remote(meta, meta_w.at[w], s_m, r_m, ((w + k) % WIDE, n)).start()
        return 0

    def send_meta_narrow(k, _):
        remote(meta, meta_n.at[n], s_mn, r_mn, (w, (n + k) % NARROW)).start()
        return 0

    lax.fori_loop(1, WIDE, send_meta, 0)
    lax.fori_loop(1, NARROW, send_meta_narrow, 0)

    others = hid_all.at[pl.ds(0, WIDE - 1)]
    all_hidden = remote(others, others, s_a, r_a, (w, n))
    all_hidden.wait_recv()
    rows = hid_all[...].reshape(WIDE * 8, hid_all.shape[2])
    part_q = jnp.dot(rows, w_query[...], preferred_element_type=F32)
    part_kv = lax.dot_general(
        rows, w_kv_t[...], (((1,), (1,)), ((), ())), preferred_element_type=F32
    )
    send_b[:, 0:32, :] = part_q.reshape(NARROW, 32, HD)
    part_kv = part_kv.reshape(NARROW, 4, 8, 32)
    for j in range(4):
        send_b[:, 32:40, 32 * j : 32 * j + 32] = part_kv[:, j]
    recv_b[pl.ds(n, 1)] = send_b[pl.ds(n, 1)]

    def send_sums(k, _):
        peer = (n + k) % NARROW
        remote(send_b.at[peer], recv_b.at[n], s_b, r_b, (w, peer)).start()
        return 0

    lax.fori_loop(1, NARROW, send_sums, 0)
    others = recv_b.at[pl.ds(0, NARROW - 1)]
    all_sums = remote(others, others, s_b, r_b, (w, n))
    all_sums.wait_recv()
    total = jnp.sum(recv_b[...], axis=0)
    q_own[...] = total[0:32].astype(BF16)
    kv_sum = total[32:40]
    for j in range(4):
        shifted = pltpu.roll(kv_sum, (y - j + 4) % 4 * 32, 1)
        kv_tiles[j] = shifted.astype(BF16)
    rows_here = pl.ds(pl.multiple_of(32 * n, 32), 32)
    one_query = remote(q_own, query_out.at[y, rows_here], s_c1, r_c1, (w, z))

    @pl.when(n != z)
    def _():
        one_query.start()

    @pl.when(hub)
    def _():
        query_out[pl.ds(y, 1), rows_here] = q_own[...][None]

    for j in range(4):
        target = NY * n + j

        @pl.when(target != w)
        def _():
            remote(kv_tiles.at[j], kv_parts.at[w], s_k1, r_k1, (target, n)).start()

        @pl.when(target == w)
        def _():
            kv_parts[pl.ds(w, 1)] = kv_tiles[j][None]

    mine = query_out.at[y]
    seven = query_out.at[y, pl.ds(0, 224)]
    parts31 = kv_parts.at[pl.ds(0, WIDE - 1)]

    @pl.when(hub)
    def _():
        remote(seven, seven, s_c1, r_c1, (w, n)).wait_recv()

        def send_query(k, _):
            peer = ((z + k) % NZ) * NY + y
            remote(mine, mine, s_c2, r_c2, (peer, n)).start()
            return 0

        lax.fori_loop(1, NZ, send_query, 0)

    @pl.when(n != z)
    def _():
        remote(mine, mine, s_c2, r_c2, (w, n)).wait_recv()

    for dy in (1, 3, 2):
        remote(mine, mine, s_c3, r_c3, (z * NY + (y + dy) % NY, n)).start()

    @pl.when(hub)
    def _():
        remote(parts31, parts31, s_k1, r_k1, (w, n)).wait_recv()
        lane = lax.broadcasted_iota(I32, (8, HD), 1)
        for b in range(8):
            merged = jnp.zeros((8, HD), F32)
            for t in range(4):
                piece = kv_parts[4 * b + t].astype(F32)
                merged = merged + jnp.where((lane >= 32 * t) & (lane < 32 * t + 32), piece, 0.0)
            kvrow_out[:, HD * b : HD * b + HD] = merged.astype(BF16)

        def send_row(k, _):
            remote(kvrow_out, kvrow_out, s_k2, r_k2, (w, (n + k) % NARROW)).start()
            return 0

        lax.fori_loop(1, NARROW, send_row, 0)

    for dx in (1, 3, 2):
        source = 2 * ((x + 4 - dx) % 4) + c
        arrived = kv_out.at[source]
        remote(arrived, arrived, s_x, r_x.at[dx - 1], (w, n)).wait_recv()
        remote(arrived, arrived, s_p, r_p.at[dx], (w, other)).start()

    @pl.when(n != z)
    def _():
        remote(kvrow_out, kvrow_out, s_k2, r_k2, (w, n)).wait_recv()

    wide_tiles = meta_w.at[pl.ds(0, WIDE - 1)]
    narrow_tiles = meta_n.at[pl.ds(0, NARROW - 1)]
    remote(wide_tiles, wide_tiles, s_m, r_m, (w, n)).wait()
    remote(narrow_tiles, narrow_tiles, s_mn, r_mn, (w, n)).wait()
    meta_wide[...] = meta_w[:, 0, :]
    meta_narrow[...] = meta_n[...]
    three = query_out.at[pl.ds(0, 3)]
    remote(three, three, s_c3, r_c3, (w, n)).wait()
    for own in own_copies:
        own.wait()
    stay.wait()
    one = kv_out.at[0]
    for i in range(4):
        remote(one, one, s_p, r_p.at[i], (w, n)).wait_recv()
    three = kv_out.at[pl.ds(0, 3)]
    remote(three, three, s_x, r_x.at[0], (w, n)).wait_send()
    four = kv_out.at[pl.ds(0, 4)]
    remote(four, four, s_p, r_p.at[0], (w, n)).wait_send()
    all_hidden.wait_send()
    all_sums.wait_send()

    @pl.when(n != z)
    def _():
        one_query.wait_send()

    three = kv_tiles.at[pl.ds(0, 3)]
    four = kv_tiles.at[pl.ds(0, 4)]

    @pl.when(hub)
    def _():
        remote(three, three, s_k1, r_k1, (w, n)).wait_send()
        seven_rows = kv_parts.at[pl.ds(0, 28)]
        row7 = query_out.at[pl.ds(0, 3)]
        row4 = query_out.at[pl.ds(0, 4)]
        remote(row7, row7, s_c2, r_c2, (w, n)).wait_send()
        remote(row4, row4, s_c2, r_c2, (w, n)).wait_send()
        for _ in range(7):
            remote(kvrow_out, kvrow_out, s_k2, r_k2, (w, n)).wait_send()

    @pl.when(n != z)
    def _():
        remote(four, four, s_k1, r_k1, (w, n)).wait_send()

    gone = moved_out.at[pl.ds(0, WIDE - 1)]
    remote(gone, gone, s_mig, r_mig, (w, n)).wait()


def payload_stats(peak, total, group, step):
    stat = jnp.where(group == step, peak, jnp.where(group - 8 == step, total, 0.0))
    first = stat.astype(BF16)
    rest = stat - first.astype(F32)
    second = rest.astype(BF16)
    third = (rest - second.astype(F32)).astype(BF16)
    return first, second, third


def attention_kernel(
    counts, meta_rows, accepted, meta_narrow, query, kvrow, kv,
    out, entries, moved_req, moved_idx,
    q_rows, token_req, scores, peaks, acc,
):
    w = lax.axis_index("wide")
    n = lax.axis_index("narrow")
    x = n // 2
    rows = WIDE * STEPS

    def moved_meta(i, _):
        for k in range(2):
            moved_req[2 * i + k] = meta_rows[i, 2 * w + k]
            moved_idx[2 * i + k] = meta_rows[i, POOL + 2 * w + k]
        return 0

    lax.fori_loop(0, WIDE, moved_meta, 0)
    step = lax.broadcasted_iota(I32, (STEPS, KVH * HD * 2), 0)
    entries[0] = jnp.where(
        step < accepted[w], kvrow[0:STEPS, :].astype(F32), 0.0
    ).astype(BF16)

    row = lax.broadcasted_iota(I32, (rows, WIDE * 8), 0).astype(F32)
    col = lax.broadcasted_iota(I32, (rows, WIDE * 8), 1).astype(F32)
    req_of_row = jnp.floor((row + 0.5) * 0.2)
    pick = (col == req_of_row * 3.0 + row).astype(F32).astype(BF16)
    for h in range(4):
        q_rows[rows * h : rows * h + rows, :] = jnp.dot(
            pick, query[h], preferred_element_type=F32
        ).astype(BF16)

    page_meta = meta_narrow[:, 1, :].astype(F32).astype(BF16)
    page = lax.broadcasted_iota(I32, (2 * POOL, POOL * PAGE), 0)
    token = lax.broadcasted_iota(I32, (2 * POOL, POOL * PAGE), 1)
    page_of = token >> 4
    spread_req = (page == page_of).astype(F32).astype(BF16)
    spread_seen = (page - POOL == page_of).astype(F32).astype(BF16)
    owner = jnp.dot(page_meta, spread_req, preferred_element_type=F32)
    seen = jnp.dot(page_meta, spread_seen, preferred_element_type=F32)
    within = (lax.broadcasted_iota(I32, (NARROW, POOL * PAGE), 1) & 15).astype(F32)
    owner = jnp.where(within < seen, owner, -1.0)
    width = CHUNK * PAGE
    per = POOL // CHUNK
    for s in range(NARROW):
        for i in range(per):
            token_req[per * s + i] = jnp.broadcast_to(
                owner[s : s + 1, width * i : width * i + width], (8, width)
            )

    peaks[...] = jnp.full(peaks.shape, NEG, F32)
    acc[...] = jnp.zeros_like(acc)
    all_row = lax.broadcasted_iota(I32, (rows, 1), 0).astype(F32)
    row_req = jnp.floor((all_row + 0.5) * 0.2)
    row_req = jnp.concatenate([row_req] * 4, axis=0)

    base = jnp.int32(0)
    bases = []
    for s in range(NARROW):
        bases.append(base)
        chunks = (counts[s, 0] + (CHUNK - 1)) // CHUNK

        def score(i, _, s=s, base=base):
            keys = kv[s, 0, pl.ds(i * CHUNK, CHUNK)].reshape(width, HD)
            raw = lax.dot_general(
                q_rows[...], keys, (((1,), (1,)), ((), ())), preferred_element_type=F32
            )
            owners = token_req[per * s + i][0:1, :]
            raw = jnp.where(row_req == owners, raw, NEG)
            scores[base + i] = raw
            peaks[...] = jnp.maximum(
                peaks[...], jnp.maximum(raw[:, 0:HD], raw[:, HD : 2 * HD])
            )
            return 0

        lax.fori_loop(0, chunks, score, 0)
        base = base + chunks

    peak = jnp.max(peaks[...], axis=1, keepdims=True)
    ones = jnp.ones((width, HD), BF16)
    for s in range(NARROW):
        chunks = (counts[s, 0] + (CHUNK - 1)) // CHUNK

        def weigh(i, _, s=s, base=bases[s]):
            values = kv[s, 1, pl.ds(i * CHUNK, CHUNK)].reshape(width, HD)
            weights = jnp.exp2((scores[base + i] - peak) * (SCALE * LOG2E)).astype(BF16)
            acc[...] += jnp.dot(
                weights, jnp.concatenate([values, ones], axis=1), preferred_element_type=F32
            )
            return 0

        lax.fori_loop(0, chunks, weigh, 0)

    slot = lax.broadcasted_iota(I32, (WIDE * 8, rows), 0)
    req_of_slot = (slot >> 3).astype(F32)
    place = (slot & 7).astype(F32)
    source = lax.broadcasted_iota(I32, (WIDE * 8, rows), 1).astype(F32)
    req_of_source = jnp.floor((source + 0.5) * 0.2)
    step_of_source = source - req_of_source * 5.0
    same = req_of_slot == req_of_source
    spread = [(same & (place == step_of_source)).astype(F32).astype(BF16)]
    for k in range(3):
        spread.append((same & (place == 5.0 + k)).astype(F32).astype(BF16))
    spread = jnp.concatenate(spread, axis=1)
    group = (lax.broadcasted_iota(I32, (rows, HD), 1) >> 3).astype(F32)
    srow = lax.broadcasted_iota(I32, (rows, HD), 0).astype(F32)
    step_of = srow - jnp.floor((srow + 0.5) * 0.2) * 5.0
    for h in range(4):
        here = slice(rows * h, rows * h + rows)
        terms = payload_stats(peak[here] * SCALE, acc[here, HD:], group, step_of)
        stacked = jnp.concatenate([acc[here, 0:HD].astype(BF16), *terms], axis=0)
        laid = jnp.dot(spread, stacked, preferred_element_type=F32)
        out[0:WIDE, h] = laid.astype(BF16).reshape(WIDE, 8, HD)

    q_new = query[:, pl.ds(pl.multiple_of(8 * w, 8), 8), :].reshape(32, HD)
    k_new = kvrow[:, pl.ds(pl.multiple_of(HD * x, HD), HD)]
    v_new = kvrow[:, pl.ds(pl.multiple_of(KVH * HD + HD * x, HD), HD)]
    fresh = lax.dot_general(
        q_new, k_new, (((1,), (1,)), ((), ())), preferred_element_type=F32
    ) * SCALE
    fresh_row = lax.broadcasted_iota(I32, (32, 8), 0) & 7
    fresh_key = lax.broadcasted_iota(I32, (32, 8), 1)
    known = fresh_key <= fresh_row
    fresh = jnp.where(known, fresh, NEG)
    fresh_peak = jnp.max(fresh, axis=1, keepdims=True)
    fresh_weight = jnp.where(known, jnp.exp(fresh - fresh_peak), 0.0)
    fresh_total = jnp.sum(fresh_weight, axis=1, keepdims=True)
    fresh_sum = jnp.dot(fresh_weight.astype(BF16), v_new, preferred_element_type=F32)
    lane_group = lax.broadcasted_iota(I32, (8, HD), 1) >> 3
    sub = lax.broadcasted_iota(I32, (8, HD), 0)
    for h in range(4):
        here = slice(8 * h, 8 * h + 8)
        stat = jnp.where(
            lane_group == sub,
            fresh_peak[here],
            jnp.where(lane_group - 8 == sub, fresh_total[here], 0.0),
        )
        line = jnp.sum(jnp.where(sub < STEPS, stat, 0.0), axis=0, keepdims=True)
        first = line.astype(BF16).astype(F32)
        second = (line - first).astype(BF16).astype(F32)
        third = line - first - second
        tile = jnp.where(
            sub < STEPS,
            fresh_sum[here],
            jnp.where(sub == 5, first, jnp.where(sub == 6, second, third)),
        )
        out[WIDE, h] = tile.astype(BF16)


def combine_kernel(
    partial, w_out, leaving,
    attended, moved_out,
    received, own, gathered, send_e, recv_e,
    s_d, r_d, s_g, r_g, s_e, r_e, s_mig, r_mig, l_sem,
):
    w = lax.axis_index("wide")
    n = lax.axis_index("narrow")
    received[pl.ds(w, 1)] = partial[pl.ds(w, 1)]
    received[WIDE] = partial[WIDE]
    enter(w, n)

    def send_partial(k, _):
        peer = (w + k) % WIDE
        remote(partial.at[peer], received.at[w], s_d, r_d, (peer, n)).start()
        return 0

    lax.fori_loop(1, WIDE, send_partial, 0)

    def send_page(k, _):
        peer = (w + k) % WIDE
        remote(leaving.at[1, peer], moved_out.at[w], s_mig, r_mig, (peer, n)).start()
        return 0

    lax.fori_loop(1, WIDE, send_page, 0)
    stay = pltpu.make_async_copy(leaving.at[1, w], moved_out.at[w], l_sem)
    stay.start()
    others = received.at[pl.ds(0, WIDE - 1)]
    all_partial = remote(others, others, s_d, r_d, (w, n))
    all_partial.wait_recv()
    sub = lax.broadcasted_iota(I32, (1, 8, HD), 1)
    group = lax.broadcasted_iota(I32, (1, 8, HD), 2) >> 3
    for h in range(4):
        tiles = received[:, h].astype(F32)
        line = (tiles[:, 7:8] + tiles[:, 6:7]) + tiles[:, 5:6]
        peak = jnp.max(jnp.where(group == sub, line, -3e38), axis=2, keepdims=True)
        total = jnp.max(jnp.where(group - 8 == sub, line, 0.0), axis=2, keepdims=True)
        top = jnp.max(peak, axis=0, keepdims=True)
        factor = jnp.exp(peak - top)
        total = jnp.sum(factor * total, axis=0)
        sums = jnp.sum(factor * tiles, axis=0)
        own[:, HD * h : HD * h + HD] = jnp.where(
            sub[0] < STEPS, sums / jnp.where(sub[0] < STEPS, total, 1.0), 0.0
        ).astype(BF16)
    gathered[pl.ds(w, 1)] = own[...][None]

    def send_own(k, _):
        remote(own, gathered.at[w], s_g, r_g, ((w + k) % WIDE, n)).start()
        return 0

    lax.fori_loop(1, WIDE, send_own, 0)
    others = gathered.at[pl.ds(0, WIDE - 1)]
    all_rows = remote(others, others, s_g, r_g, (w, n))
    all_rows.wait_recv()
    rows = gathered[...].reshape(WIDE * 8, gathered.shape[2])
    product = jnp.dot(rows, w_out[...], preferred_element_type=F32)
    send_e[...] = product.astype(BF16).reshape(NARROW, 32, HD)
    recv_e[pl.ds(n, 1)] = send_e[pl.ds(n, 1)]

    def send_product(k, _):
        peer = (n + k) % NARROW
        remote(send_e.at[peer], recv_e.at[n], s_e, r_e, (w, peer)).start()
        return 0

    lax.fori_loop(1, NARROW, send_product, 0)
    others = recv_e.at[pl.ds(0, NARROW - 1)]
    all_products = remote(others, others, s_e, r_e, (w, n))
    all_products.wait_recv()
    total = jnp.sum(recv_e[...].astype(F32), axis=0)
    for j in range(4):
        attended[STEPS * j : STEPS * j + STEPS, :] = total[8 * j : 8 * j + STEPS].astype(BF16)
    all_partial.wait_send()
    all_rows.wait_send()
    all_products.wait_send()
    stay.wait()
    gone = moved_out.at[pl.ds(0, WIDE - 1)]
    remote(gone, gone, s_mig, r_mig, (w, n)).wait()


def on_device(hidden, w_query, w_keyval, w_out, pool, page_req, page_idx, lengths, moves, accepted):
    dma = pltpu.SemaphoreType.DMA
    shape = jax.ShapeDtypeStruct
    page_shape = pool.shape[1:]
    leaving, pages, meta = pl.pallas_call(
        sort_kernel,
        out_shape=(
            shape((2, WIDE) + page_shape, BF16),
            shape(pool.shape, BF16),
            shape((8, 128), I32),
        ),
        in_specs=[SMEM_SPEC] * 4 + [ANY_SPEC],
        out_specs=(ANY_SPEC, ANY_SPEC, SMEM_SPEC),
        scratch_shapes=[pltpu.SMEM((WIDE,), I32), dma((2,))],
        name="sort_pages",
    )(moves.reshape(POOL), page_req, page_idx, lengths, pool)

    depth = hidden.shape[1]
    query, kvrow, kv, moved_a, meta_wide, meta_narrow = pl.pallas_call(
        gather_kernel,
        out_shape=(
            shape((4, WIDE * 8, HD), BF16),
            shape((8, 1024), BF16),
            shape((NARROW, 2, POOL, PAGE, HD), BF16),
            shape((WIDE,) + page_shape, BF16),
            shape((WIDE, 128), I32),
            shape((NARROW, 8, 128), I32),
        ),
        in_specs=[VMEM_SPEC] * 4 + [ANY_SPEC] * 2,
        out_specs=(VMEM_SPEC, VMEM_SPEC, ANY_SPEC, ANY_SPEC, VMEM_SPEC, VMEM_SPEC),
        scratch_shapes=[
            pltpu.VMEM((8, depth), BF16),
            pltpu.VMEM((WIDE, 8, depth), BF16),
            pltpu.VMEM((NARROW, 40, HD), F32),
            pltpu.VMEM((NARROW, 40, HD), F32),
            pltpu.VMEM((32, HD), BF16),
            pltpu.VMEM((4, 8, HD), BF16),
            pltpu.VMEM((WIDE, 8, HD), BF16),
            pltpu.VMEM((WIDE, 8, 128), I32),
            pltpu.VMEM((NARROW, 8, 128), I32),
            dma, dma, dma, dma, dma, dma, dma, dma,
            dma((3,)), dma, dma((3,)), dma, dma((4,)),
            dma, dma, dma, dma, dma, dma, dma, dma, dma, dma, dma, dma,
        ],
        compiler_params=pltpu.CompilerParams(collective_id=0, has_side_effects=True),
        name="spread_queries",
    )(hidden, w_query, w_keyval.T, meta, leaving, pages)

    rows = 4 * WIDE * STEPS
    width = CHUNK * PAGE
    chunks = NARROW * POOL // CHUNK
    partial, entries, moved_req, moved_idx = pl.pallas_call(
        attention_kernel,
        out_shape=(
            shape((WIDE + 1, 4, 8, HD), BF16),
            shape((1, STEPS, 1024), BF16),
            shape((POOL,), I32),
            shape((POOL,), I32),
        ),
        in_specs=[SMEM_SPEC] * 3 + [VMEM_SPEC] * 4,
        out_specs=(VMEM_SPEC, VMEM_SPEC, SMEM_SPEC, SMEM_SPEC),
        scratch_shapes=[
            pltpu.VMEM((rows, HD), BF16),
            pltpu.VMEM((chunks, 8, width), F32),
            pltpu.VMEM((chunks, rows, width), F32),
            pltpu.VMEM((rows, HD), F32),
            pltpu.VMEM((rows, 2 * HD), F32),
        ],
        compiler_params=pltpu.CompilerParams(vmem_limit_bytes=48 << 20),
        name="attend",
    )(meta_narrow[:, 2, 0:1], meta_wide, accepted, meta_narrow, query, kvrow, kv)

    attended, moved_b = pl.pallas_call(
        combine_kernel,
        out_shape=(
            shape((4 * STEPS, HD), BF16),
            shape((WIDE,) + page_shape, BF16),
        ),
        in_specs=[VMEM_SPEC] * 2 + [ANY_SPEC],
        out_specs=(VMEM_SPEC, ANY_SPEC),
        scratch_shapes=[
            pltpu.VMEM((WIDE + 1, 4, 8, HD), BF16),
            pltpu.VMEM((8, 4 * HD), BF16),
            pltpu.VMEM((WIDE, 8, 4 * HD), BF16),
            pltpu.VMEM((NARROW, 32, HD), BF16),
            pltpu.VMEM((NARROW, 32, HD), BF16),
            dma, dma, dma, dma, dma, dma, dma, dma, dma,
        ],
        compiler_params=pltpu.CompilerParams(collective_id=1, has_side_effects=True),
        name="combine",
    )(partial, w_out, leaving)
    moved = jnp.stack([moved_a, moved_b], axis=1).reshape(pool.shape)
    return attended, entries, moved, moved_req, moved_idx


def solution(mesh):
    in_specs = (
        P("wide", "narrow"),
        P("narrow", "wide"),
        P("narrow", "wide"),
        P("narrow", "wide"),
        P(("wide", "narrow"), None, None),
        P(("wide", "narrow")),
        P(("wide", "narrow")),
        P(),
        P(("wide", "narrow"), None),
        P(),
    )
    out_specs = (
        P("narrow", "wide"),
        P("wide", None, None),
        P(("wide", "narrow"), None, None),
        P(("wide", "narrow")),
        P(("wide", "narrow")),
    )
    return jax.shard_map(
        on_device, mesh=mesh, in_specs=in_specs, out_specs=out_specs, check_vma=False
    )
```

```python
import functools
import math

import jax
import jax.numpy as jnp
from jax import lax
from jax.experimental import pallas as pl
from jax.experimental.pallas import tpu as pltpu
from jax.sharding import PartitionSpec as P

HEADS = 32
KVH = 4
HD = 128
STEPS = 5
PAGE = 16
WIDE = 32
NARROW = 8
NY = 4
NZ = 8
POOL = 64
CHUNK = 16
SCALE = 1.0 / math.sqrt(HD)
LOG2E = 1.4426950408889634
NEG = -1e30
F32 = jnp.float32
BF16 = jnp.bfloat16
I32 = jnp.int32
MESH = pl.DeviceIdType.MESH
VMEM_SPEC = pl.BlockSpec(memory_space=pltpu.VMEM)
SMEM_SPEC = pl.BlockSpec(memory_space=pltpu.SMEM)
ANY_SPEC = pl.BlockSpec(memory_space=pl.ANY)


def sort_kernel(moves, req, idx, lens, pool, first_out, second_out, live_out, meta, count):
    def clear(d, _):
        count[d] = 0
        return 0

    lax.fori_loop(0, WIDE, clear, 0)

    def place(p, state):
        live, free = state
        d = moves[p]
        k = count[d]
        count[d] = k + 1
        r = req[p]
        i = idx[p]
        page = pool[p]

        @pl.when(k == 0)
        def _():
            first_out[d] = page

        @pl.when(k != 0)
        def _():
            second_out[d] = page

        meta[0, 2 * d + k] = r
        meta[0, POOL + 2 * d + k] = i
        alive = r >= 0
        pos = jnp.where(alive, live, POOL - 1 - free)
        live_out[pos] = page
        seen = jnp.clip(lens[jnp.maximum(r, 0)] - i * PAGE, 0, PAGE)
        meta[1, pos] = r
        meta[1, POOL + pos] = jnp.where(alive, seen, 0)
        step = jnp.where(alive, 1, 0)
        return live + step, free + 1 - step

    live, _ = lax.fori_loop(0, POOL, place, (jnp.int32(0), jnp.int32(0)))
    meta[2, 0] = live


def enter(w, n):
    barrier = pltpu.get_barrier_semaphore()

    def wide_signal(k, _):
        pl.semaphore_signal(
            barrier, inc=1, device_id=((w + k) % WIDE, n), device_id_type=MESH
        )
        return 0

    def narrow_signal(k, _):
        pl.semaphore_signal(
            barrier, inc=1, device_id=(w, (n + k) % NARROW), device_id_type=MESH
        )
        return 0

    lax.fori_loop(1, WIDE, wide_signal, 0)
    lax.fori_loop(1, NARROW, narrow_signal, 0)
    pl.semaphore_wait(barrier, WIDE + NARROW - 2)


def remote(src, dst, send, recv, device):
    return pltpu.make_async_remote_copy(
        src_ref=src,
        dst_ref=dst,
        send_sem=send,
        recv_sem=recv,
        device_id=device,
        device_id_type=MESH,
    )


def gather_kernel(
    hidden, w_query, w_kv_t, meta, leaving, pages,
    query_out, kvrow_out, kv_out, moved_out, meta_wide, meta_narrow,
    hid_own, hid_all, send_b, recv_b, q_own, kv_tiles, kv_parts, meta_w, meta_n,
    s_a, r_a, s_m, r_m, s_mn, r_mn, s_mig, r_mig, l_sem, s_x, r_x, s_p, r_p,
    s_b, r_b, s_c1, r_c1, s_k1, r_k1, s_c2, r_c2, s_k2, r_k2, s_c3, r_c3,
):
    w = lax.axis_index("wide")
    n = lax.axis_index("narrow")
    z = w // NY
    y = w % NY
    x = n // 2
    c = n % 2
    other = 2 * x + (1 - c)
    hub = n == z
    hid_own[...] = jnp.zeros_like(hid_own)
    hid_own[0:STEPS, :] = hidden[...]
    hid_all[pl.ds(w, 1)] = hid_own[...][None]
    meta_w[pl.ds(w, 1)] = meta[...][None]
    meta_n[pl.ds(n, 1)] = meta[...][None]
    enter(w, n)

    def send_hidden(k, _):
        remote(hid_own, hid_all.at[w], s_a, r_a, ((w + k) % WIDE, n)).start()
        return 0

    lax.fori_loop(1, WIDE, send_hidden, 0)

    def key_block(head):
        return pl.ds(pl.multiple_of(HD * head, HD), HD)

    def value_block(head):
        return pl.ds(pl.multiple_of(KVH * HD + HD * head, HD), HD)

    for dx in (1, 3, 2):
        tx = (x + dx) % 4
        for part, block in ((0, key_block(tx)), (1, value_block(tx))):
            remote(
                pages.at[:, :, block], kv_out.at[n, part], s_x, r_x.at[dx - 1], (w, 2 * tx + c)
            ).start()
    own_copies = []
    for part, block in ((0, key_block(x)), (1, value_block(x))):
        remote(pages.at[:, :, block], kv_out.at[n, part], s_p, r_p.at[0], (w, other)).start()
        own = pltpu.make_async_copy(pages.at[:, :, block], kv_out.at[n, part], l_sem.at[part])
        own.start()
        own_copies.append(own)

    def send_page(k, _):
        peer = (w + k) % WIDE
        remote(leaving.at[peer], moved_out.at[w], s_mig, r_mig, (peer, n)).start()
        return 0

    lax.fori_loop(1, WIDE, send_page, 0)
    stay = pltpu.make_async_copy(leaving.at[w], moved_out.at[w], l_sem.at[2])
    stay.start()

    def send_meta(k, _):
        remote(meta, meta_w.at[w], s_m, r_m, ((w + k) % WIDE, n)).start()
        return 0

    def send_meta_narrow(k, _):
        remote(meta, meta_n.at[n], s_mn, r_mn, (w, (n + k) % NARROW)).start()
        return 0

    lax.fori_loop(1, WIDE, send_meta, 0)
    lax.fori_loop(1, NARROW, send_meta_narrow, 0)

    others = hid_all.at[pl.ds(0, WIDE - 1)]
    all_hidden = remote(others, others, s_a, r_a, (w, n))
    all_hidden.wait_recv()
    rows = hid_all[...].reshape(WIDE * 8, hid_all.shape[2])
    part_q = jnp.dot(rows, w_query[...], preferred_element_type=F32)
    part_kv = lax.dot_general(
        rows, w_kv_t[...], (((1,), (1,)), ((), ())), preferred_element_type=F32
    )
    send_b[:, 0:32, :] = part_q.reshape(NARROW, 32, HD)
    part_kv = part_kv.reshape(NARROW, 4, 8, 32)
    for j in range(4):
        send_b[:, 32:40, 32 * j : 32 * j + 32] = part_kv[:, j]
    recv_b[pl.ds(n, 1)] = send_b[pl.ds(n, 1)]

    def send_sums(k, _):
        peer = (n + k) % NARROW
        remote(send_b.at[peer], recv_b.at[n], s_b, r_b, (w, peer)).start()
        return 0

    lax.fori_loop(1, NARROW, send_sums, 0)
    others = recv_b.at[pl.ds(0, NARROW - 1)]
    all_sums = remote(others, others, s_b, r_b, (w, n))
    all_sums.wait_recv()
    total = jnp.sum(recv_b[...], axis=0)
    q_own[...] = total[0:32].astype(BF16)
    kv_sum = total[32:40]
    for j in range(4):
        shifted = pltpu.roll(kv_sum, (y - j + 4) % 4 * 32, 1)
        kv_tiles[j] = shifted.astype(BF16)
    rows_here = pl.ds(pl.multiple_of(32 * n, 32), 32)
    one_query = remote(q_own, query_out.at[y, rows_here], s_c1, r_c1, (w, z))

    @pl.when(n != z)
    def _():
        one_query.start()

    @pl.when(hub)
    def _():
        query_out[pl.ds(y, 1), rows_here] = q_own[...][None]

    for j in range(4):
        target = NY * n + j

        @pl.when(target != w)
        def _():
            remote(kv_tiles.at[j], kv_parts.at[w], s_k1, r_k1, (target, n)).start()

        @pl.when(target == w)
        def _():
            kv_parts[pl.ds(w, 1)] = kv_tiles[j][None]

    mine = query_out.at[y]
    seven = query_out.at[y, pl.ds(0, 224)]
    parts31 = kv_parts.at[pl.ds(0, WIDE - 1)]

    @pl.when(hub)
    def _():
        remote(seven, seven, s_c1, r_c1, (w, n)).wait_recv()

        def send_query(k, _):
            peer = ((z + k) % NZ) * NY + y
            remote(mine, mine, s_c2, r_c2, (peer, n)).start()
            return 0

        lax.fori_loop(1, NZ, send_query, 0)

    @pl.when(n != z)
    def _():
        remote(mine, mine, s_c2, r_c2, (w, n)).wait_recv()

    for dy in (1, 3, 2):
        remote(mine, mine, s_c3, r_c3, (z * NY + (y + dy) % NY, n)).start()

    @pl.when(hub)
    def _():
        remote(parts31, parts31, s_k1, r_k1, (w, n)).wait_recv()
        lane = lax.broadcasted_iota(I32, (8, HD), 1)
        for b in range(8):
            merged = jnp.zeros((8, HD), F32)
            for t in range(4):
                piece = kv_parts[4 * b + t].astype(F32)
                merged = merged + jnp.where((lane >= 32 * t) & (lane < 32 * t + 32), piece, 0.0)
            kvrow_out[:, HD * b : HD * b + HD] = merged.astype(BF16)

        def send_row(k, _):
            remote(kvrow_out, kvrow_out, s_k2, r_k2, (w, (n + k) % NARROW)).start()
            return 0

        lax.fori_loop(1, NARROW, send_row, 0)

    for dx in (1, 3, 2):
        source = 2 * ((x + 4 - dx) % 4) + c
        arrived = kv_out.at[source]
        remote(arrived, arrived, s_x, r_x.at[dx - 1], (w, n)).wait_recv()
        remote(arrived, arrived, s_p, r_p.at[dx], (w, other)).start()

    @pl.when(n != z)
    def _():
        remote(kvrow_out, kvrow_out, s_k2, r_k2, (w, n)).wait_recv()

    wide_tiles = meta_w.at[pl.ds(0, WIDE - 1)]
    narrow_tiles = meta_n.at[pl.ds(0, NARROW - 1)]
    remote(wide_tiles, wide_tiles, s_m, r_m, (w, n)).wait()
    remote(narrow_tiles, narrow_tiles, s_mn, r_mn, (w, n)).wait()
    meta_wide[...] = meta_w[:, 0, :]
    meta_narrow[...] = meta_n[...]
    three = query_out.at[pl.ds(0, 3)]
    remote(three, three, s_c3, r_c3, (w, n)).wait()
    for own in own_copies:
        own.wait()
    stay.wait()
    one = kv_out.at[0]
    for i in range(4):
        remote(one, one, s_p, r_p.at[i], (w, n)).wait_recv()
    three = kv_out.at[pl.ds(0, 3)]
    remote(three, three, s_x, r_x.at[0], (w, n)).wait_send()
    four = kv_out.at[pl.ds(0, 4)]
    remote(four, four, s_p, r_p.at[0], (w, n)).wait_send()
    all_hidden.wait_send()
    all_sums.wait_send()

    @pl.when(n != z)
    def _():
        one_query.wait_send()

    three = kv_tiles.at[pl.ds(0, 3)]
    four = kv_tiles.at[pl.ds(0, 4)]

    @pl.when(hub)
    def _():
        remote(three, three, s_k1, r_k1, (w, n)).wait_send()
        seven_rows = kv_parts.at[pl.ds(0, 28)]
        row7 = query_out.at[pl.ds(0, 3)]
        row4 = query_out.at[pl.ds(0, 4)]
        remote(row7, row7, s_c2, r_c2, (w, n)).wait_send()
        remote(row4, row4, s_c2, r_c2, (w, n)).wait_send()
        for _ in range(7):
            remote(kvrow_out, kvrow_out, s_k2, r_k2, (w, n)).wait_send()

    @pl.when(n != z)
    def _():
        remote(four, four, s_k1, r_k1, (w, n)).wait_send()

    gone = moved_out.at[pl.ds(0, WIDE - 1)]
    remote(gone, gone, s_mig, r_mig, (w, n)).wait()


def payload_stats(peak, total, group, step):
    stat = jnp.where(group == step, peak, jnp.where(group - 8 == step, total, 0.0))
    first = stat.astype(BF16)
    rest = stat - first.astype(F32)
    second = rest.astype(BF16)
    third = (rest - second.astype(F32)).astype(BF16)
    return first, second, third


def attention_kernel(
    counts, meta_rows, accepted, meta_narrow, query, kvrow, kv,
    out, entries, moved_req, moved_idx,
    q_rows, token_req, scores, peaks, acc,
):
    w = lax.axis_index("wide")
    n = lax.axis_index("narrow")
    x = n // 2
    rows = WIDE * STEPS

    def moved_meta(i, _):
        for k in range(2):
            moved_req[2 * i + k] = meta_rows[i, 2 * w + k]
            moved_idx[2 * i + k] = meta_rows[i, POOL + 2 * w + k]
        return 0

    lax.fori_loop(0, WIDE, moved_meta, 0)
    step = lax.broadcasted_iota(I32, (STEPS, KVH * HD * 2), 0)
    entries[0] = jnp.where(
        step < accepted[w], kvrow[0:STEPS, :].astype(F32), 0.0
    ).astype(BF16)

    row = lax.broadcasted_iota(I32, (rows, WIDE * 8), 0).astype(F32)
    col = lax.broadcasted_iota(I32, (rows, WIDE * 8), 1).astype(F32)
    req_of_row = jnp.floor((row + 0.5) * 0.2)
    pick = (col == req_of_row * 3.0 + row).astype(F32).astype(BF16)
    for h in range(4):
        q_rows[rows * h : rows * h + rows, :] = jnp.dot(
            pick, query[h], preferred_element_type=F32
        ).astype(BF16)

    page_meta = meta_narrow[:, 1, :].astype(F32).astype(BF16)
    page = lax.broadcasted_iota(I32, (2 * POOL, POOL * PAGE), 0)
    token = lax.broadcasted_iota(I32, (2 * POOL, POOL * PAGE), 1)
    page_of = token >> 4
    spread_req = (page == page_of).astype(F32).astype(BF16)
    spread_seen = (page - POOL == page_of).astype(F32).astype(BF16)
    owner = jnp.dot(page_meta, spread_req, preferred_element_type=F32)
    seen = jnp.dot(page_meta, spread_seen, preferred_element_type=F32)
    within = (lax.broadcasted_iota(I32, (NARROW, POOL * PAGE), 1) & 15).astype(F32)
    owner = jnp.where(within < seen, owner, -1.0)
    width = CHUNK * PAGE
    per = POOL // CHUNK
    for s in range(NARROW):
        for i in range(per):
            token_req[per * s + i] = jnp.broadcast_to(
                owner[s : s + 1, width * i : width * i + width], (8, width)
            )

    peaks[...] = jnp.full(peaks.shape, NEG, F32)
    acc[...] = jnp.zeros_like(acc)
    all_row = lax.broadcasted_iota(I32, (rows, 1), 0).astype(F32)
    row_req = jnp.floor((all_row + 0.5) * 0.2)
    row_req = jnp.concatenate([row_req] * 4, axis=0)

    base = jnp.int32(0)
    bases = []
    for s in range(NARROW):
        bases.append(base)
        chunks = (counts[s, 0] + (CHUNK - 1)) // CHUNK

        def score(i, _, s=s, base=base):
            keys = kv[s, 0, pl.ds(i * CHUNK, CHUNK)].reshape(width, HD)
            raw = lax.dot_general(
                q_rows[...], keys, (((1,), (1,)), ((), ())), preferred_element_type=F32
            )
            owners = token_req[per * s + i][0:1, :]
            raw = jnp.where(row_req == owners, raw, NEG)
            scores[base + i] = raw
            peaks[...] = jnp.maximum(
                peaks[...], jnp.maximum(raw[:, 0:HD], raw[:, HD : 2 * HD])
            )
            return 0

        lax.fori_loop(0, chunks, score, 0)
        base = base + chunks

    peak = jnp.max(peaks[...], axis=1, keepdims=True)
    ones = jnp.ones((width, HD), BF16)
    for s in range(NARROW):
        chunks = (counts[s, 0] + (CHUNK - 1)) // CHUNK

        def weigh(i, _, s=s, base=bases[s]):
            values = kv[s, 1, pl.ds(i * CHUNK, CHUNK)].reshape(width, HD)
            weights = jnp.exp2((scores[base + i] - peak) * (SCALE * LOG2E)).astype(BF16)
            acc[...] += jnp.dot(
                weights, jnp.concatenate([values, ones], axis=1), preferred_element_type=F32
            )
            return 0

        lax.fori_loop(0, chunks, weigh, 0)

    slot = lax.broadcasted_iota(I32, (WIDE * 8, rows), 0)
    req_of_slot = (slot >> 3).astype(F32)
    place = (slot & 7).astype(F32)
    source = lax.broadcasted_iota(I32, (WIDE * 8, rows), 1).astype(F32)
    req_of_source = jnp.floor((source + 0.5) * 0.2)
    step_of_source = source - req_of_source * 5.0
    same = req_of_slot == req_of_source
    spread = [(same & (place == step_of_source)).astype(F32).astype(BF16)]
    for k in range(3):
        spread.append((same & (place == 5.0 + k)).astype(F32).astype(BF16))
    spread = jnp.concatenate(spread, axis=1)
    group = (lax.broadcasted_iota(I32, (rows, HD), 1) >> 3).astype(F32)
    srow = lax.broadcasted_iota(I32, (rows, HD), 0).astype(F32)
    step_of = srow - jnp.floor((srow + 0.5) * 0.2) * 5.0
    for h in range(4):
        here = slice(rows * h, rows * h + rows)
        terms = payload_stats(peak[here] * SCALE, acc[here, HD:], group, step_of)
        stacked = jnp.concatenate([acc[here, 0:HD].astype(BF16), *terms], axis=0)
        laid = jnp.dot(spread, stacked, preferred_element_type=F32)
        out[0:WIDE, h] = laid.astype(BF16).reshape(WIDE, 8, HD)

    q_new = query[:, pl.ds(pl.multiple_of(8 * w, 8), 8), :].reshape(32, HD)
    k_new = kvrow[:, pl.ds(pl.multiple_of(HD * x, HD), HD)]
    v_new = kvrow[:, pl.ds(pl.multiple_of(KVH * HD + HD * x, HD), HD)]
    fresh = lax.dot_general(
        q_new, k_new, (((1,), (1,)), ((), ())), preferred_element_type=F32
    ) * SCALE
    fresh_row = lax.broadcasted_iota(I32, (32, 8), 0) & 7
    fresh_key = lax.broadcasted_iota(I32, (32, 8), 1)
    known = fresh_key <= fresh_row
    fresh = jnp.where(known, fresh, NEG)
    fresh_peak = jnp.max(fresh, axis=1, keepdims=True)
    fresh_weight = jnp.where(known, jnp.exp(fresh - fresh_peak), 0.0)
    fresh_total = jnp.sum(fresh_weight, axis=1, keepdims=True)
    fresh_sum = jnp.dot(fresh_weight.astype(BF16), v_new, preferred_element_type=F32)
    lane_group = lax.broadcasted_iota(I32, (8, HD), 1) >> 3
    sub = lax.broadcasted_iota(I32, (8, HD), 0)
    for h in range(4):
        here = slice(8 * h, 8 * h + 8)
        stat = jnp.where(
            lane_group == sub,
            fresh_peak[here],
            jnp.where(lane_group - 8 == sub, fresh_total[here], 0.0),
        )
        line = jnp.sum(jnp.where(sub < STEPS, stat, 0.0), axis=0, keepdims=True)
        first = line.astype(BF16).astype(F32)
        second = (line - first).astype(BF16).astype(F32)
        third = line - first - second
        tile = jnp.where(
            sub < STEPS,
            fresh_sum[here],
            jnp.where(sub == 5, first, jnp.where(sub == 6, second, third)),
        )
        out[WIDE, h] = tile.astype(BF16)


def combine_kernel(
    partial, w_out, leaving,
    attended, moved_out,
    received, own, gathered, send_e, recv_e,
    s_d, r_d, s_g, r_g, s_e, r_e, s_mig, r_mig, l_sem,
):
    w = lax.axis_index("wide")
    n = lax.axis_index("narrow")
    received[pl.ds(w, 1)] = partial[pl.ds(w, 1)]
    received[WIDE] = partial[WIDE]
    enter(w, n)

    def send_partial(k, _):
        peer = (w + k) % WIDE
        remote(partial.at[peer], received.at[w], s_d, r_d, (peer, n)).start()
        return 0

    lax.fori_loop(1, WIDE, send_partial, 0)

    def send_page(k, _):
        peer = (w + k) % WIDE
        remote(leaving.at[peer], moved_out.at[w], s_mig, r_mig, (peer, n)).start()
        return 0

    lax.fori_loop(1, WIDE, send_page, 0)
    stay = pltpu.make_async_copy(leaving.at[w], moved_out.at[w], l_sem)
    stay.start()
    others = received.at[pl.ds(0, WIDE - 1)]
    all_partial = remote(others, others, s_d, r_d, (w, n))
    all_partial.wait_recv()
    sub = lax.broadcasted_iota(I32, (1, 8, HD), 1)
    group = lax.broadcasted_iota(I32, (1, 8, HD), 2) >> 3
    for h in range(4):
        tiles = received[:, h].astype(F32)
        line = (tiles[:, 7:8] + tiles[:, 6:7]) + tiles[:, 5:6]
        peak = jnp.max(jnp.where(group == sub, line, -3e38), axis=2, keepdims=True)
        total = jnp.max(jnp.where(group - 8 == sub, line, 0.0), axis=2, keepdims=True)
        top = jnp.max(peak, axis=0, keepdims=True)
        factor = jnp.exp(peak - top)
        total = jnp.sum(factor * total, axis=0)
        sums = jnp.sum(factor * tiles, axis=0)
        own[:, HD * h : HD * h + HD] = jnp.where(
            sub[0] < STEPS, sums / jnp.where(sub[0] < STEPS, total, 1.0), 0.0
        ).astype(BF16)
    gathered[pl.ds(w, 1)] = own[...][None]

    def send_own(k, _):
        remote(own, gathered.at[w], s_g, r_g, ((w + k) % WIDE, n)).start()
        return 0

    lax.fori_loop(1, WIDE, send_own, 0)
    others = gathered.at[pl.ds(0, WIDE - 1)]
    all_rows = remote(others, others, s_g, r_g, (w, n))
    all_rows.wait_recv()
    rows = gathered[...].reshape(WIDE * 8, gathered.shape[2])
    product = jnp.dot(rows, w_out[...], preferred_element_type=F32)
    send_e[...] = product.astype(BF16).reshape(NARROW, 32, HD)
    recv_e[pl.ds(n, 1)] = send_e[pl.ds(n, 1)]

    def send_product(k, _):
        peer = (n + k) % NARROW
        remote(send_e.at[peer], recv_e.at[n], s_e, r_e, (w, peer)).start()
        return 0

    lax.fori_loop(1, NARROW, send_product, 0)
    others = recv_e.at[pl.ds(0, NARROW - 1)]
    all_products = remote(others, others, s_e, r_e, (w, n))
    all_products.wait_recv()
    total = jnp.sum(recv_e[...].astype(F32), axis=0)
    for j in range(4):
        attended[STEPS * j : STEPS * j + STEPS, :] = total[8 * j : 8 * j + STEPS].astype(BF16)
    all_partial.wait_send()
    all_rows.wait_send()
    all_products.wait_send()
    stay.wait()
    gone = moved_out.at[pl.ds(0, WIDE - 1)]
    remote(gone, gone, s_mig, r_mig, (w, n)).wait()


def on_device(hidden, w_query, w_keyval, w_out, pool, page_req, page_idx, lengths, moves, accepted):
    dma = pltpu.SemaphoreType.DMA
    shape = jax.ShapeDtypeStruct
    page_shape = pool.shape[1:]
    first, second, pages, meta = pl.pallas_call(
        sort_kernel,
        out_shape=(
            shape((WIDE,) + page_shape, BF16),
            shape((WIDE,) + page_shape, BF16),
            shape(pool.shape, BF16),
            shape((8, 128), I32),
        ),
        in_specs=[SMEM_SPEC] * 4 + [VMEM_SPEC],
        out_specs=(VMEM_SPEC, VMEM_SPEC, VMEM_SPEC, SMEM_SPEC),
        scratch_shapes=[pltpu.SMEM((WIDE,), I32)],
        name="sort_pages",
    )(moves.reshape(POOL), page_req, page_idx, lengths, pool)

    depth = hidden.shape[1]
    query, kvrow, kv, moved_a, meta_wide, meta_narrow = pl.pallas_call(
        gather_kernel,
        out_shape=(
            shape((4, WIDE * 8, HD), BF16),
            shape((8, 1024), BF16),
            shape((NARROW, 2, POOL, PAGE, HD), BF16),
            shape((WIDE,) + page_shape, BF16),
            shape((WIDE, 128), I32),
            shape((NARROW, 8, 128), I32),
        ),
        in_specs=[VMEM_SPEC] * 4 + [ANY_SPEC] * 2,
        out_specs=(VMEM_SPEC, VMEM_SPEC, ANY_SPEC, ANY_SPEC, VMEM_SPEC, VMEM_SPEC),
        scratch_shapes=[
            pltpu.VMEM((8, depth), BF16),
            pltpu.VMEM((WIDE, 8, depth), BF16),
            pltpu.VMEM((NARROW, 40, HD), F32),
            pltpu.VMEM((NARROW, 40, HD), F32),
            pltpu.VMEM((32, HD), BF16),
            pltpu.VMEM((4, 8, HD), BF16),
            pltpu.VMEM((WIDE, 8, HD), BF16),
            pltpu.VMEM((WIDE, 8, 128), I32),
            pltpu.VMEM((NARROW, 8, 128), I32),
            dma, dma, dma, dma, dma, dma, dma, dma,
            dma((3,)), dma, dma((3,)), dma, dma((4,)),
            dma, dma, dma, dma, dma, dma, dma, dma, dma, dma, dma, dma,
        ],
        compiler_params=pltpu.CompilerParams(collective_id=0, has_side_effects=True),
        name="spread_queries",
    )(hidden, w_query, w_keyval.T, meta, first, pages)

    rows = 4 * WIDE * STEPS
    width = CHUNK * PAGE
    chunks = NARROW * POOL // CHUNK
    partial, entries, moved_req, moved_idx = pl.pallas_call(
        attention_kernel,
        out_shape=(
            shape((WIDE + 1, 4, 8, HD), BF16),
            shape((1, STEPS, 1024), BF16),
            shape((POOL,), I32),
            shape((POOL,), I32),
        ),
        in_specs=[SMEM_SPEC] * 3 + [VMEM_SPEC] * 4,
        out_specs=(VMEM_SPEC, VMEM_SPEC, SMEM_SPEC, SMEM_SPEC),
        scratch_shapes=[
            pltpu.VMEM((rows, HD), BF16),
            pltpu.VMEM((chunks, 8, width), F32),
            pltpu.VMEM((chunks, rows, width), F32),
            pltpu.VMEM((rows, HD), F32),
            pltpu.VMEM((rows, 2 * HD), F32),
        ],
        compiler_params=pltpu.CompilerParams(vmem_limit_bytes=48 << 20),
        name="attend",
    )(meta_narrow[:, 2, 0:1], meta_wide, accepted, meta_narrow, query, kvrow, kv)

    attended, moved_b = pl.pallas_call(
        combine_kernel,
        out_shape=(
            shape((4 * STEPS, HD), BF16),
            shape((WIDE,) + page_shape, BF16),
        ),
        in_specs=[VMEM_SPEC] * 2 + [ANY_SPEC],
        out_specs=(VMEM_SPEC, ANY_SPEC),
        scratch_shapes=[
            pltpu.VMEM((WIDE + 1, 4, 8, HD), BF16),
            pltpu.VMEM((8, 4 * HD), BF16),
            pltpu.VMEM((WIDE, 8, 4 * HD), BF16),
            pltpu.VMEM((NARROW, 32, HD), BF16),
            pltpu.VMEM((NARROW, 32, HD), BF16),
            dma, dma, dma, dma, dma, dma, dma, dma, dma,
        ],
        compiler_params=pltpu.CompilerParams(collective_id=1, has_side_effects=True),
        name="combine",
    )(partial, w_out, second)
    moved = jnp.stack([moved_a, moved_b], axis=1).reshape(pool.shape)
    return attended, entries, moved, moved_req, moved_idx


def solution(mesh):
    in_specs = (
        P("wide", "narrow"),
        P("narrow", "wide"),
        P("narrow", "wide"),
        P("narrow", "wide"),
        P(("wide", "narrow"), None, None),
        P(("wide", "narrow")),
        P(("wide", "narrow")),
        P(),
        P(("wide", "narrow"), None),
        P(),
    )
    out_specs = (
        P("narrow", "wide"),
        P("wide", None, None),
        P(("wide", "narrow"), None, None),
        P(("wide", "narrow")),
        P(("wide", "narrow")),
    )
    return jax.shard_map(
        on_device, mesh=mesh, in_specs=in_specs, out_specs=out_specs, check_vma=False
    )
```

```python
import functools
import math

import jax
import jax.numpy as jnp
from jax import lax
from jax.experimental import pallas as pl
from jax.experimental.pallas import tpu as pltpu
from jax.sharding import PartitionSpec as P

HEADS = 32
KVH = 4
HD = 128
STEPS = 5
PAGE = 16
WIDE = 32
NARROW = 8
NY = 4
NZ = 8
POOL = 64
CHUNK = 32
EARLY = ((1, 0), (3, 0))
LATE = ((1, 1), (3, 1), (2, 0), (2, 1))
ORDER = (0, 1, 3, 2)
CUT1 = 5
CUT2 = 12
CUT3 = 12
SCALE = 1.0 / math.sqrt(HD)
LOG2E = 1.4426950408889634
NEG = -1e30
F32 = jnp.float32
BF16 = jnp.bfloat16
I32 = jnp.int32
MESH = pl.DeviceIdType.MESH
VMEM_SPEC = pl.BlockSpec(memory_space=pltpu.VMEM)
SMEM_SPEC = pl.BlockSpec(memory_space=pltpu.SMEM)
ANY_SPEC = pl.BlockSpec(memory_space=pl.ANY)


def order_kernel(moves, req, idx, lens, source, meta, count):
    def clear(d, _):
        count[d] = 0
        return 0

    lax.fori_loop(0, WIDE, clear, 0)

    def place(p, _):
        d = moves[p]
        k = count[d]
        count[d] = k + 1
        r = req[p]
        i = idx[p]
        source[2 * d + k] = p
        meta[0, 2 * d + k] = r
        meta[0, POOL + 2 * d + k] = i
        seen = jnp.clip(lens[jnp.maximum(r, 0)] - i * PAGE, 0, PAGE)
        meta[1, p] = r
        meta[1, POOL + p] = jnp.where(r >= 0, seen, 0)
        return 0

    lax.fori_loop(0, POOL, place, 0)


def enter(w, n):
    barrier = pltpu.get_barrier_semaphore()

    def wide_signal(k, _):
        pl.semaphore_signal(
            barrier, inc=1, device_id=((w + k) % WIDE, n), device_id_type=MESH
        )
        return 0

    def narrow_signal(k, _):
        pl.semaphore_signal(
            barrier, inc=1, device_id=(w, (n + k) % NARROW), device_id_type=MESH
        )
        return 0

    lax.fori_loop(1, WIDE, wide_signal, 0)
    lax.fori_loop(1, NARROW, narrow_signal, 0)
    pl.semaphore_wait(barrier, WIDE + NARROW - 2)


def remote(src, dst, send, recv, device):
    return pltpu.make_async_remote_copy(
        src_ref=src,
        dst_ref=dst,
        send_sem=send,
        recv_sem=recv,
        device_id=device,
        device_id_type=MESH,
    )


def payload_stats(peak, total, group, step):
    stat = jnp.where(group == step, peak, jnp.where(group - 8 == step, total, 0.0))
    first = stat.astype(BF16)
    rest = stat - first.astype(F32)
    second = rest.astype(BF16)
    third = (rest - second.astype(F32)).astype(BF16)
    return first, second, third


def whole_kernel(
    source, accepted, hidden, w_query, w_kv_t, w_out, meta, pool,
    attended, entries, moved_out, moved_req, moved_idx,
    hid_own, hid_all, part_q, part_kv, sum_q, sum_kv, query, kv_tiles, kv_four, kv_new,
    meta_w, meta_n, meta_s, pool_v, leaving, kv, pick, spread,
    token_req, scores, peaks, acc, partial, received, own, gathered, send_e, recv_e,
    s_a, r_a, s_m, r_m, s_mn, r_mn, s_mig, r_mig, l_sem, s_x, r_x, s_p, r_p,
    s_b, r_b, s_bk, r_bk, s_k1, r_k1, s_c2, r_c2, s_k2, r_k2, s_c3, r_c3,
    s_d, r_d, s_g, r_g, s_e, r_e,
):
    w = lax.axis_index("wide")
    n = lax.axis_index("narrow")
    z = w // NY
    y = w % NY
    x = n // 2
    c = n % 2
    other = 2 * x + (1 - c)
    rows = WIDE * STEPS
    load_pool = pltpu.make_async_copy(pool, pool_v, l_sem.at[0])
    load_pool.start()
    hid_own[...] = jnp.zeros_like(hid_own)
    hid_own[0:STEPS, :] = hidden[...]
    hid_all[pl.ds(w, 1)] = hid_own[...][None]
    meta_w[pl.ds(w, 1)] = meta[...][None]
    meta_n[pl.ds(n, 1)] = meta[...][None]
    enter(w, n)

    def send_hidden(k, _):
        remote(hid_own, hid_all.at[w], s_a, r_a, ((w + k) % WIDE, n)).start()
        return 0

    lax.fori_loop(1, WIDE, send_hidden, 0)

    def send_meta(k, _):
        remote(meta, meta_w.at[w], s_m, r_m, ((w + k) % WIDE, n)).start()
        return 0

    def send_meta_narrow(k, _):
        remote(meta, meta_n.at[n], s_mn, r_mn, (w, (n + k) % NARROW)).start()
        return 0

    lax.fori_loop(1, NARROW, send_meta_narrow, 0)

    def block_of(part, head):
        return pl.ds(pl.multiple_of(KVH * HD * part + HD * head, HD), HD)

    def exchange(dx, part):
        tx = (x + dx) % 4
        remote(
            pool.at[:, :, block_of(part, tx)],
            kv.at[n, part],
            s_x,
            r_x.at[dx - 1, part],
            (w, 2 * tx + c),
        ).start()

    own_copies = []
    for part in range(2):
        mine_here = pool.at[:, :, block_of(part, x)]
        remote(mine_here, kv.at[n, part], s_p, r_p.at[0], (w, other)).start()
        copy = pltpu.make_async_copy(mine_here, kv.at[n, part], l_sem.at[1 + part])
        copy.start()
        own_copies.append(copy)
    for dx, part in EARLY:
        exchange(dx, part)

    row = lax.broadcasted_iota(I32, (rows, WIDE * 8), 0).astype(F32)
    col = lax.broadcasted_iota(I32, (rows, WIDE * 8), 1).astype(F32)
    req_of_row = jnp.floor((row + 0.5) * 0.2)
    pick[...] = (col == req_of_row * 3.0 + row).astype(F32).astype(BF16)
    slot = lax.broadcasted_iota(I32, (WIDE * 8, rows), 0)
    req_of_slot = (slot >> 3).astype(F32)
    place = (slot & 7).astype(F32)
    origin = lax.broadcasted_iota(I32, (WIDE * 8, rows), 1).astype(F32)
    req_of_origin = jnp.floor((origin + 0.5) * 0.2)
    step_of_origin = origin - req_of_origin * 5.0
    same = req_of_slot == req_of_origin
    spread[0] = (same & (place == step_of_origin)).astype(F32).astype(BF16)
    for k in range(3):
        spread[1 + k] = (same & (place == 5.0 + k)).astype(F32).astype(BF16)
    peaks[...] = jnp.full(peaks.shape, NEG, F32)
    acc[...] = jnp.zeros_like(acc)

    load_pool.wait()

    def take_page(j, _):
        leaving[j] = pool_v[source[j]]
        return 0

    lax.fori_loop(0, POOL, take_page, 0)
    stay = pltpu.make_async_copy(
        leaving.at[pl.ds(2 * w, 2)], moved_out.at[pl.ds(2 * w, 2)], l_sem.at[3]
    )
    stay.start()

    def send_pages(first, last):
        def send_pair(i, _):
            for k in (i, WIDE - i):
                peer = (w + k) % WIDE
                remote(
                    leaving.at[pl.ds(2 * peer, 2)],
                    moved_out.at[pl.ds(2 * w, 2)],
                    s_mig,
                    r_mig,
                    (peer, n),
                ).start()
            return 0

        lax.fori_loop(first, min(last, 16), send_pair, 0)
        if first <= 16 < last:
            peer = (w + 16) % WIDE
            remote(
                leaving.at[pl.ds(2 * peer, 2)],
                moved_out.at[pl.ds(2 * w, 2)],
                s_mig,
                r_mig,
                (peer, n),
            ).start()

    others = hid_all.at[pl.ds(0, WIDE - 1)]
    all_hidden = remote(others, others, s_a, r_a, (w, n))
    all_hidden.wait_recv()
    padded = hid_all[...].reshape(WIDE * 8, hid_all.shape[2])
    packed = jnp.dot(pick[...], padded, preferred_element_type=F32).astype(BF16)
    part_q[...] = jnp.dot(packed, w_query[...], preferred_element_type=F32)
    to_hub_q = remote(part_q, sum_q.at[n], s_b, r_b, (w, z))
    to_hub_kv = remote(part_kv, sum_kv.at[n], s_bk, r_bk, (w, z))

    @pl.when(n != z)
    def _():
        to_hub_q.start()

    new_kv = lax.dot_general(
        padded, w_kv_t[...], (((1,), (1,)), ((), ())), preferred_element_type=F32
    )
    for j in range(4):
        part_kv[:, 32 * j : 32 * j + 32] = new_kv[64 * j : 64 * j + 64]

    @pl.when(n != z)
    def _():
        to_hub_kv.start()

    for dx, part in LATE:
        exchange(dx, part)
    lax.fori_loop(1, WIDE, send_meta, 0)
    send_pages(1, CUT1)
    mine = query.at[y]
    seven_q = sum_q.at[pl.ds(0, 7)]
    seven_kv = sum_kv.at[pl.ds(0, 7)]

    @pl.when(n == z)
    def _():
        sum_q[pl.ds(n, 1)] = part_q[...][None]
        remote(seven_q, seven_q, s_b, r_b, (w, n)).wait_recv()
        query[pl.ds(y, 1)] = jnp.sum(sum_q[...], axis=0).astype(BF16)[None]

        def send_query(k, _):
            peer = ((z + k) % NZ) * NY + y
            remote(mine, mine, s_c2, r_c2, (peer, n)).start()
            return 0

        lax.fori_loop(1, NZ, send_query, 0)

    @pl.when(n != z)
    def _():
        remote(mine, mine, s_c2, r_c2, (w, n)).wait_recv()

    for dy in (1, 3, 2):
        remote(mine, mine, s_c3, r_c3, (z * NY + (y + dy) % NY, n)).start()

    @pl.when(n == z)
    def _():
        sum_kv[pl.ds(n, 1)] = part_kv[...][None]
        remote(seven_kv, seven_kv, s_bk, r_bk, (w, n)).wait_recv()
        kv_tiles[...] = jnp.sum(sum_kv[...], axis=0).astype(BF16).reshape(8, 8, HD)
        kv_four[pl.ds(y, 1)] = kv_tiles[pl.ds(w % 8, 1)]

        def send_tile(k, _):
            peer = (w + k) % WIDE
            remote(kv_tiles.at[peer % 8], kv_four.at[y], s_k1, r_k1, (peer, n)).start()
            return 0

        lax.fori_loop(1, WIDE, send_tile, 0)

    send_pages(CUT1, CUT2)

    def relay(dx):
        arrived = 2 * ((x + 4 - dx) % 4) + c
        for part in range(2):
            here = kv.at[arrived, part]
            remote(here, here, s_x, r_x.at[dx - 1, part], (w, n)).wait_recv()
        here = kv.at[arrived]
        remote(here, here, s_p, r_p.at[dx], (w, other)).start()

    relay(1)
    relay(3)
    narrow_tiles = meta_n.at[pl.ds(0, NARROW - 1)]
    remote(narrow_tiles, narrow_tiles, s_mn, r_mn, (w, n)).wait()
    page_meta = meta_n[:, 1, :].astype(F32).astype(BF16)
    page = lax.broadcasted_iota(I32, (2 * POOL, POOL * PAGE), 0)
    page_of = lax.broadcasted_iota(I32, (2 * POOL, POOL * PAGE), 1) >> 4
    spread_req = (page == page_of).astype(F32).astype(BF16)
    spread_seen = (page - POOL == page_of).astype(F32).astype(BF16)
    owner = jnp.dot(page_meta, spread_req, preferred_element_type=F32)
    seen = jnp.dot(page_meta, spread_seen, preferred_element_type=F32)
    within = (lax.broadcasted_iota(I32, (NARROW, POOL * PAGE), 1) & 15).astype(F32)
    owner = jnp.where(within < seen, owner, -1.0)
    width = CHUNK * PAGE
    per = POOL // CHUNK
    for s in range(NARROW):
        for i in range(per):
            token_req[per * s + i] = jnp.broadcast_to(
                owner[s : s + 1, width * i : width * i + width], (8, width)
            )
    all_row = lax.broadcasted_iota(I32, (rows, 1), 0).astype(F32)
    row_req = jnp.floor((all_row + 0.5) * 0.2)
    row_req = jnp.concatenate([row_req] * 4, axis=0)
    three = query.at[pl.ds(0, 3)]
    spread_query = remote(three, three, s_c3, r_c3, (w, n))
    spread_query.wait_recv()

    for copy in own_copies:
        copy.wait()
    for g, dx in enumerate(ORDER):
        if dx == 2:
            relay(2)
        from_other = kv.at[2 * ((x + 4 - dx) % 4) + (1 - c)]
        remote(from_other, from_other, s_p, r_p.at[dx], (w, n)).wait_recv()

        def score(j, _, g=g, dx=dx):
            s = 2 * ((x + 4 - dx) % 4) + j // per
            i = j % per
            keys = kv[s, 0, pl.ds(i * CHUNK, CHUNK)].reshape(width, HD)
            raw = lax.dot_general(
                query[...].reshape(4 * rows, HD),
                keys,
                (((1,), (1,)), ((), ())),
                preferred_element_type=F32,
            )
            owners = token_req[per * s + i][0:1, :]
            raw = jnp.where(row_req == owners, raw, NEG)
            scores[2 * per * g + j] = raw
            top = raw[:, 0:HD]
            for t in range(1, width // HD):
                top = jnp.maximum(top, raw[:, HD * t : HD * t + HD])
            peaks[...] = jnp.maximum(peaks[...], top)
            return 0

        lax.fori_loop(0, 2 * per, score, 0)

    peak = jnp.max(peaks[...], axis=1, keepdims=True)
    ones = jnp.ones((width, HD), BF16)
    for g, dx in enumerate(ORDER):

        def weigh(j, _, g=g, dx=dx):
            s = 2 * ((x + 4 - dx) % 4) + j // per
            i = j % per
            values = kv[s, 1, pl.ds(i * CHUNK, CHUNK)].reshape(width, HD)
            weights = jnp.exp2(
                (scores[2 * per * g + j] - peak) * (SCALE * LOG2E)
            ).astype(BF16)
            acc[...] += jnp.dot(
                weights, jnp.concatenate([values, ones], axis=1), preferred_element_type=F32
            )
            return 0

        lax.fori_loop(0, 2 * per, weigh, 0)

    group = (lax.broadcasted_iota(I32, (rows, HD), 1) >> 3).astype(F32)
    srow = lax.broadcasted_iota(I32, (rows, HD), 0).astype(F32)
    step_of = srow - jnp.floor((srow + 0.5) * 0.2) * 5.0
    for h in range(4):
        here = slice(rows * h, rows * h + rows)
        terms = payload_stats(peak[here] * SCALE, acc[here, HD:], group, step_of)
        laid = jnp.dot(spread[0], acc[here, 0:HD].astype(BF16), preferred_element_type=F32)
        for k in range(3):
            laid += jnp.dot(spread[1 + k], terms[k], preferred_element_type=F32)
        partial[:, h] = laid.astype(BF16).reshape(WIDE, 8, HD)

    def send_partial(k, _):
        peer = (w + k) % WIDE
        remote(partial.at[peer], received.at[w], s_d, r_d, (peer, n)).start()
        return 0

    lax.fori_loop(1, WIDE, send_partial, 0)
    received[pl.ds(w, 1)] = partial[pl.ds(w, 1)]
    send_pages(CUT2, CUT3)

    four_tiles = kv_four
    three_tiles = kv_four.at[pl.ds(0, 3)]

    @pl.when(n != z)
    def _():
        remote(four_tiles, four_tiles, s_k1, r_k1, (w, n)).wait_recv()

    @pl.when(n == z)
    def _():
        remote(three_tiles, three_tiles, s_k1, r_k1, (w, n)).wait_recv()

    lane = lax.broadcasted_iota(I32, (8, HD), 1)
    merged = jnp.zeros((8, HD), F32)
    for t in range(4):
        turned = pltpu.roll(kv_four[t].astype(F32), (t + 4 - w // 8) % 4 * 32, 1)
        merged = merged + jnp.where((lane >= 32 * t) & (lane < 32 * t + 32), turned, 0.0)
    kv_new[pl.ds(n, 1)] = merged.astype(BF16)[None]

    def send_new(k, _):
        remote(kv_new.at[n], kv_new.at[n], s_k2, r_k2, (w, (n + k) % NARROW)).start()
        return 0

    lax.fori_loop(1, NARROW, send_new, 0)
    wide_tiles = meta_w.at[pl.ds(0, WIDE - 1)]
    remote(wide_tiles, wide_tiles, s_m, r_m, (w, n)).wait()
    to_scalar = pltpu.make_async_copy(meta_w.at[:, 0], meta_s, l_sem.at[4])
    to_scalar.start()
    to_scalar.wait()

    def moved_meta(i, _):
        for k in range(2):
            moved_req[2 * i + k] = meta_s[i, 2 * w + k]
            moved_idx[2 * i + k] = meta_s[i, POOL + 2 * w + k]
        return 0

    lax.fori_loop(0, WIDE, moved_meta, 0)
    seven_new = kv_new.at[pl.ds(0, 7)]
    remote(seven_new, seven_new, s_k2, r_k2, (w, n)).wait()
    step = lax.broadcasted_iota(I32, (STEPS, HD), 0)
    for b in range(8):
        entries[0, :, HD * b : HD * b + HD] = jnp.where(
            step < accepted[w], kv_new[b][0:STEPS, :].astype(F32), 0.0
        ).astype(BF16)

    first_row = lax.broadcasted_iota(I32, (32, rows), 0)
    from_row = lax.broadcasted_iota(I32, (32, rows), 1)
    ours = (from_row == 5 * w + (first_row & 7)) & ((first_row & 7) < STEPS)
    ours = ours.astype(F32).astype(BF16)
    k_new = kv_new[x]
    v_new = kv_new[KVH + x]
    sub = lax.broadcasted_iota(I32, (8, HD), 0)
    lane_group = lane >> 3
    fresh_row = lax.broadcasted_iota(I32, (8, 8), 0)
    fresh_key = lax.broadcasted_iota(I32, (8, 8), 1)
    known = fresh_key <= fresh_row
    for h in range(4):
        q_new = jnp.dot(ours[0:8], query[h], preferred_element_type=F32).astype(BF16)
        fresh = lax.dot_general(
            q_new, k_new, (((1,), (1,)), ((), ())), preferred_element_type=F32
        ) * SCALE
        fresh = jnp.where(known, fresh, NEG)
        fresh_peak = jnp.max(fresh, axis=1, keepdims=True)
        fresh_weight = jnp.where(known, jnp.exp(fresh - fresh_peak), 0.0)
        fresh_total = jnp.sum(fresh_weight, axis=1, keepdims=True)
        fresh_sum = jnp.dot(fresh_weight.astype(BF16), v_new, preferred_element_type=F32)
        stat = jnp.where(
            lane_group == sub,
            fresh_peak,
            jnp.where(lane_group - 8 == sub, fresh_total, 0.0),
        )
        line = jnp.sum(jnp.where(sub < STEPS, stat, 0.0), axis=0, keepdims=True)
        first = line.astype(BF16).astype(F32)
        second = (line - first).astype(BF16).astype(F32)
        third = line - first - second
        tile = jnp.where(
            sub < STEPS,
            fresh_sum,
            jnp.where(sub == 5, first, jnp.where(sub == 6, second, third)),
        )
        received[WIDE, h] = tile.astype(BF16)

    others = received.at[pl.ds(0, WIDE - 1)]
    all_partial = remote(others, others, s_d, r_d, (w, n))
    all_partial.wait_recv()
    sub3 = lax.broadcasted_iota(I32, (1, 8, HD), 1)
    group3 = lax.broadcasted_iota(I32, (1, 8, HD), 2) >> 3
    for h in range(4):
        tiles = received[:, h].astype(F32)
        line = (tiles[:, 7:8] + tiles[:, 6:7]) + tiles[:, 5:6]
        high = jnp.max(jnp.where(group3 == sub3, line, -3e38), axis=2, keepdims=True)
        total = jnp.max(jnp.where(group3 - 8 == sub3, line, 0.0), axis=2, keepdims=True)
        top = jnp.max(high, axis=0, keepdims=True)
        factor = jnp.exp(high - top)
        total = jnp.sum(factor * total, axis=0)
        sums = jnp.sum(factor * tiles, axis=0)
        own[:, HD * h : HD * h + HD] = jnp.where(
            sub < STEPS, sums / jnp.where(sub < STEPS, total, 1.0), 0.0
        ).astype(BF16)
    gathered[pl.ds(w, 1)] = own[...][None]

    def send_own(k, _):
        remote(own, gathered.at[w], s_g, r_g, ((w + k) % WIDE, n)).start()
        return 0

    lax.fori_loop(1, WIDE, send_own, 0)
    send_pages(CUT3, 17)
    others = gathered.at[pl.ds(0, WIDE - 1)]
    all_rows = remote(others, others, s_g, r_g, (w, n))
    all_rows.wait_recv()
    attn = gathered[...].reshape(WIDE * 8, gathered.shape[2])
    product = jnp.dot(attn, w_out[...], preferred_element_type=F32)
    send_e[...] = product.astype(BF16).reshape(NARROW, 32, HD)
    recv_e[pl.ds(n, 1)] = send_e[pl.ds(n, 1)]

    def send_product(k, _):
        peer = (n + k) % NARROW
        remote(send_e.at[peer], recv_e.at[n], s_e, r_e, (w, peer)).start()
        return 0

    lax.fori_loop(1, NARROW, send_product, 0)
    others = recv_e.at[pl.ds(0, NARROW - 1)]
    all_products = remote(others, others, s_e, r_e, (w, n))
    all_products.wait_recv()
    result = jnp.sum(recv_e[...].astype(F32), axis=0)
    for j in range(4):
        attended[STEPS * j : STEPS * j + STEPS, :] = result[8 * j : 8 * j + STEPS].astype(BF16)

    all_hidden.wait_send()
    spread_query.wait_send()
    three = kv.at[pl.ds(0, 3)]
    remote(three, three, s_x, r_x.at[0, 0], (w, n)).wait_send()
    four = kv.at[pl.ds(0, 4)]
    remote(four, four, s_p, r_p.at[0], (w, n)).wait_send()

    @pl.when(n != z)
    def _():
        to_hub_q.wait_send()
        to_hub_kv.wait_send()

    tiles31 = received.at[pl.ds(0, 31), 0]

    @pl.when(n == z)
    def _():
        remote(tiles31, tiles31, s_k1, r_k1, (w, n)).wait_send()
        four_q = query
        three_q = query.at[pl.ds(0, 3)]
        remote(four_q, four_q, s_c2, r_c2, (w, n)).wait_send()
        remote(three_q, three_q, s_c2, r_c2, (w, n)).wait_send()

    all_partial.wait_send()
    all_rows.wait_send()
    all_products.wait_send()
    stay.wait()
    gone = moved_out.at[pl.ds(0, POOL - 2)]
    remote(gone, gone, s_mig, r_mig, (w, n)).wait()


def on_device(hidden, w_query, w_keyval, w_out, pool, page_req, page_idx, lengths, moves, accepted):
    dma = pltpu.SemaphoreType.DMA
    shape = jax.ShapeDtypeStruct
    source, meta = pl.pallas_call(
        order_kernel,
        out_shape=(shape((POOL,), I32), shape((8, 128), I32)),
        in_specs=[SMEM_SPEC] * 4,
        out_specs=(SMEM_SPEC, SMEM_SPEC),
        scratch_shapes=[pltpu.SMEM((WIDE,), I32)],
        name="order_pages",
    )(moves.reshape(POOL), page_req, page_idx, lengths)

    depth = hidden.shape[1]
    rows = WIDE * STEPS
    width = CHUNK * PAGE
    chunks = NARROW * POOL // CHUNK
    attended, entries, moved, moved_req, moved_idx = pl.pallas_call(
        whole_kernel,
        out_shape=(
            shape((4 * STEPS, HD), BF16),
            shape((1, STEPS, 1024), BF16),
            shape(pool.shape, BF16),
            shape((POOL,), I32),
            shape((POOL,), I32),
        ),
        in_specs=[SMEM_SPEC] * 2 + [VMEM_SPEC] * 5 + [ANY_SPEC],
        out_specs=(VMEM_SPEC, VMEM_SPEC, ANY_SPEC, SMEM_SPEC, SMEM_SPEC),
        scratch_shapes=[
            pltpu.VMEM((8, depth), BF16),
            pltpu.VMEM((WIDE, 8, depth), BF16),
            pltpu.VMEM((rows, HD), F32),
            pltpu.VMEM((64, HD), F32),
            pltpu.VMEM((NARROW, rows, HD), F32),
            pltpu.VMEM((NARROW, 64, HD), F32),
            pltpu.VMEM((4, rows, HD), BF16),
            pltpu.VMEM((8, 8, HD), BF16),
            pltpu.VMEM((4, 8, HD), BF16),
            pltpu.VMEM((8, 8, HD), BF16),
            pltpu.VMEM((WIDE, 8, 128), I32),
            pltpu.VMEM((NARROW, 8, 128), I32),
            pltpu.SMEM((WIDE, 128), I32),
            pltpu.VMEM(pool.shape, BF16),
            pltpu.VMEM(pool.shape, BF16),
            pltpu.VMEM((NARROW, 2, POOL, PAGE, HD), BF16),
            pltpu.VMEM((rows, WIDE * 8), BF16),
            pltpu.VMEM((4, WIDE * 8, rows), BF16),
            pltpu.VMEM((chunks, 8, width), F32),
            pltpu.VMEM((chunks, 4 * rows, width), F32),
            pltpu.VMEM((4 * rows, HD), F32),
            pltpu.VMEM((4 * rows, 2 * HD), F32),
            pltpu.VMEM((WIDE, 4, 8, HD), BF16),
            pltpu.VMEM((WIDE + 1, 4, 8, HD), BF16),
            pltpu.VMEM((8, 4 * HD), BF16),
            pltpu.VMEM((WIDE, 8, 4 * HD), BF16),
            pltpu.VMEM((NARROW, 32, HD), BF16),
            pltpu.VMEM((NARROW, 32, HD), BF16),
            dma, dma, dma, dma, dma, dma, dma, dma,
            dma((5,)), dma, dma((3, 2)), dma, dma((4,)),
            dma, dma, dma, dma, dma, dma, dma, dma, dma, dma, dma, dma,
            dma, dma, dma, dma, dma, dma,
        ],
        compiler_params=pltpu.CompilerParams(
            collective_id=0, has_side_effects=True, vmem_limit_bytes=50 << 20
        ),
        name="verify_step",
    )(source, accepted, hidden, w_query, w_keyval.T, w_out, meta, pool)
    return attended, entries, moved, moved_req, moved_idx


def solution(mesh):
    in_specs = (
        P("wide", "narrow"),
        P("narrow", "wide"),
        P("narrow", "wide"),
        P("narrow", "wide"),
        P(("wide", "narrow"), None, None),
        P(("wide", "narrow")),
        P(("wide", "narrow")),
        P(),
        P(("wide", "narrow"), None),
        P(),
    )
    out_specs = (
        P("narrow", "wide"),
        P("wide", None, None),
        P(("wide", "narrow"), None, None),
        P(("wide", "narrow")),
        P(("wide", "narrow")),
    )
    return jax.shard_map(
        on_device, mesh=mesh, in_specs=in_specs, out_specs=out_specs, check_vma=False
    )
```

```python
import functools
import math

import jax
import jax.numpy as jnp
from jax import lax
from jax.experimental import pallas as pl
from jax.experimental.pallas import tpu as pltpu
from jax.sharding import PartitionSpec as P

HEADS = 32
KVH = 4
HD = 128
STEPS = 5
PAGE = 16
WIDE = 32
NARROW = 8
NY = 4
NZ = 8
POOL = 64
CHUNK = 32
PIECES = 4
EARLY = ((2, 0), (1, 0), (3, 0))
LATE = ((2, 1), (1, 1), (3, 1))
ORDER = (0, 2, 1, 3)
CUT1 = 8
CUT2 = 14
CUT3 = 14
SCALE = 1.0 / math.sqrt(HD)
LOG2E = 1.4426950408889634
NEG = -1e30
F32 = jnp.float32
BF16 = jnp.bfloat16
I32 = jnp.int32
MESH = pl.DeviceIdType.MESH
VMEM_SPEC = pl.BlockSpec(memory_space=pltpu.VMEM)
SMEM_SPEC = pl.BlockSpec(memory_space=pltpu.SMEM)
ANY_SPEC = pl.BlockSpec(memory_space=pl.ANY)


def greet(w, n, barrier):

    def wide_signal(k, _):
        pl.semaphore_signal(
            barrier, inc=1, device_id=((w + k) % WIDE, n), device_id_type=MESH
        )
        return 0

    def narrow_signal(k, _):
        pl.semaphore_signal(
            barrier, inc=1, device_id=(w, (n + k) % NARROW), device_id_type=MESH
        )
        return 0

    lax.fori_loop(1, WIDE, wide_signal, 0)
    lax.fori_loop(1, NARROW, narrow_signal, 0)


def remote(src, dst, send, recv, device):
    return pltpu.make_async_remote_copy(
        src_ref=src,
        dst_ref=dst,
        send_sem=send,
        recv_sem=recv,
        device_id=device,
        device_id_type=MESH,
    )


def payload_stats(peak, total, group, step):
    stat = jnp.where(group == step, peak, jnp.where(group - 8 == step, total, 0.0))
    first = stat.astype(BF16)
    rest = stat - first.astype(F32)
    second = rest.astype(BF16)
    third = (rest - second.astype(F32)).astype(BF16)
    return first, second, third


def whole_kernel(
    moves, page_req, page_idx, lengths, accepted, hidden, w_query_in, w_kv_in, w_out_in, pool,
    attended, entries, moved_out, moved_req, moved_idx,
    small, small_len, hid_in, w_query, w_kv_t, w_out, meta, source_v, source,
    hid_own, hid_all, part_q, part_kv, sum_q, sum_kv, query, kv_tiles, kv_four, kv_new,
    meta_n, pool_v, leaving, kv, pick, spread,
    token_req, scores, peaks, acc, partial, received, own, gathered, send_e, recv_e,
    l_in, s_a, r_a, s_mn, r_mn, s_mig, r_mig, l_sem, s_x, r_x, s_p, r_p,
    s_b, r_b, s_bk, r_bk, s_k1, r_k1, s_k3, r_k3, s_c2, r_c2, s_k2, r_k2, s_c3, r_c3,
    s_d, r_d, s_g, r_g, s_e, r_e,
):
    w = lax.axis_index("wide")
    n = lax.axis_index("narrow")
    z = w // NY
    y = w % NY
    x = n // 2
    c = n % 2
    other = 2 * x + (1 - c)
    rows = WIDE * STEPS
    loads = []
    for i, (origin, target) in enumerate(
        (
            (moves, small.at[0]),
            (page_req, small.at[1]),
            (page_idx, small.at[2]),
            (lengths, small_len.at[0]),
            (accepted, small_len.at[1]),
            (hidden, hid_in),
            (pool, pool_v),
            (w_query_in, w_query),
            (w_kv_in, w_kv_t),
            (w_out_in, w_out),
        )
    ):
        loads.append(pltpu.make_async_copy(origin, target, l_in.at[i]))
        loads[-1].start()
    barrier = pltpu.get_barrier_semaphore()
    greet(w, n, barrier)
    for load in loads[0:6]:
        load.wait()
    hid_own[...] = jnp.zeros_like(hid_own)
    hid_own[0:STEPS, :] = hid_in[...]
    sub64 = lax.broadcasted_iota(I32, (POOL, POOL), 0).astype(F32)
    lane64 = lax.broadcasted_iota(I32, (POOL, POOL), 1).astype(F32)
    diagonal = sub64 == lane64

    def as_column(line):
        return jnp.sum(jnp.where(diagonal, line, 0.0), axis=1, keepdims=True)

    leave = small[0].astype(F32)
    leave_column = as_column(leave)
    earlier = (leave_column == leave) & (lane64 < sub64)
    rank = jnp.sum(earlier.astype(F32), axis=1, keepdims=True)
    taken = leave_column * 2.0 + rank == lane64
    req_line = small[1].astype(F32)
    idx_line = small[2].astype(F32)

    def reorder(line):
        return jnp.sum(jnp.where(taken, as_column(line), 0.0), axis=0, keepdims=True)

    source_row = jnp.sum(jnp.where(taken, sub64, 0.0), axis=0, keepdims=True).astype(I32)
    source_v[...] = jnp.zeros_like(source_v)
    source_v[0:1, 0:POOL] = source_row
    sub32 = lax.broadcasted_iota(I32, (WIDE, WIDE), 0)
    lane32 = lax.broadcasted_iota(I32, (WIDE, WIDE), 1)
    len_column = jnp.sum(
        jnp.where(sub32 == lane32, small_len[0].astype(F32), 0.0), axis=1, keepdims=True
    )
    owner_is = lax.broadcasted_iota(I32, (WIDE, POOL), 0).astype(F32) == req_line
    length_of = jnp.sum(jnp.where(owner_is, len_column, 0.0), axis=0, keepdims=True)
    seen_line = jnp.clip(length_of - idx_line * PAGE, 0.0, float(PAGE))
    seen_line = jnp.where(req_line >= 0.0, seen_line, 0.0)
    meta[...] = jnp.zeros_like(meta)
    idx_high = jnp.floor(idx_line * (1.0 / 16.0))
    hid_own[5:6, 0:POOL] = reorder(req_line).astype(BF16)
    hid_own[6:7, 0:POOL] = reorder(idx_high).astype(BF16)
    hid_own[7:8, 0:POOL] = reorder(idx_line - idx_high * 16.0).astype(BF16)
    meta[1:2, 0:POOL] = req_line.astype(I32)
    meta[1:2, POOL : 2 * POOL] = seen_line.astype(I32)
    lane_w = lax.broadcasted_iota(I32, (1, WIDE), 1)
    accepted_here = jnp.sum(
        jnp.where(lane_w == w, small_len[1].astype(F32), 0.0), axis=1, keepdims=True
    )
    to_scalar = pltpu.make_async_copy(source_v, source, l_in.at[10])
    to_scalar.start()
    hid_all[pl.ds(w, 1)] = hid_own[...][None]
    meta_n[pl.ds(n, 1)] = meta[...][None]
    pl.semaphore_wait(barrier, WIDE + NARROW - 2)

    def block_of(part, head):
        return pl.ds(pl.multiple_of(KVH * HD * part + HD * head, HD), HD)

    def exchange(dx, part):
        tx = (x + dx) % 4
        remote(
            pool.at[:, :, block_of(part, tx)],
            kv.at[n, part],
            s_x,
            r_x.at[dx - 1, part],
            (w, 2 * tx + c),
        ).start()

    for dx, part in EARLY:
        exchange(dx, part)

    def send_hidden(k, _):
        remote(hid_own, hid_all.at[w], s_a, r_a, ((w + k) % WIDE, n)).start()
        return 0

    lax.fori_loop(1, WIDE, send_hidden, 0)

    def send_meta_narrow(k, _):
        remote(meta, meta_n.at[n], s_mn, r_mn, (w, (n + k) % NARROW)).start()
        return 0

    lax.fori_loop(1, NARROW, send_meta_narrow, 0)

    for part in range(2):
        mine_here = pool.at[:, :, block_of(part, x)]
        remote(mine_here, kv.at[n, part], s_p, r_p.at[0, part], (w, other)).start()
    row = lax.broadcasted_iota(I32, (rows, WIDE * 8), 0).astype(F32)
    col = lax.broadcasted_iota(I32, (rows, WIDE * 8), 1).astype(F32)
    req_of_row = jnp.floor((row + 0.5) * 0.2)
    pick[...] = (col == req_of_row * 3.0 + row).astype(F32).astype(BF16)
    slot = lax.broadcasted_iota(I32, (WIDE * 8, rows), 0)
    req_of_slot = (slot >> 3).astype(F32)
    place = (slot & 7).astype(F32)
    origin = lax.broadcasted_iota(I32, (WIDE * 8, rows), 1).astype(F32)
    req_of_origin = jnp.floor((origin + 0.5) * 0.2)
    step_of_origin = origin - req_of_origin * 5.0
    same = req_of_slot == req_of_origin
    spread[0] = (same & (place == step_of_origin)).astype(F32).astype(BF16)
    for k in range(3):
        spread[1 + k] = (same & (place == 5.0 + k)).astype(F32).astype(BF16)
    peaks[...] = jnp.full(peaks.shape, NEG, F32)
    acc[...] = jnp.zeros_like(acc)

    to_scalar.wait()
    loads[6].wait()

    def take_page(j, _):
        leaving[j] = pool_v[jnp.clip(source[0, j], 0, POOL - 1)]
        for part in range(2):
            kv[n, part, j] = pool_v[j, :, block_of(part, x)]
        return 0

    lax.fori_loop(0, POOL, take_page, 0)
    stay = pltpu.make_async_copy(
        leaving.at[pl.ds(2 * w, 2)], moved_out.at[pl.ds(2 * w, 2)], l_sem.at[3]
    )
    stay.start()

    def send_pages(first, last):
        def send_pair(i, _):
            for k in (i, WIDE - i):
                peer = (w + k) % WIDE
                remote(
                    leaving.at[pl.ds(2 * peer, 2)],
                    moved_out.at[pl.ds(2 * w, 2)],
                    s_mig,
                    r_mig,
                    (peer, n),
                ).start()
            return 0

        lax.fori_loop(first, min(last, 16), send_pair, 0)
        if first <= 16 < last:
            peer = (w + 16) % WIDE
            remote(
                leaving.at[pl.ds(2 * peer, 2)],
                moved_out.at[pl.ds(2 * w, 2)],
                s_mig,
                r_mig,
                (peer, n),
            ).start()

    others = hid_all.at[pl.ds(0, WIDE - 1)]
    all_hidden = remote(others, others, s_a, r_a, (w, n))
    all_hidden.wait_recv()
    padded = hid_all[...].reshape(WIDE * 8, hid_all.shape[2])
    loads[7].wait()
    loads[8].wait()
    packed = jnp.dot(pick[...], padded, preferred_element_type=F32).astype(BF16)
    part_q[...] = jnp.dot(packed, w_query[...], preferred_element_type=F32).astype(BF16)
    to_hub_q = remote(part_q, sum_q.at[n], s_b, r_b, (w, z))
    to_hub_kv = remote(part_kv, sum_kv.at[n], s_bk, r_bk, (w, z))

    @pl.when(n != z)
    def _():
        to_hub_q.start()

    new_kv = lax.dot_general(
        padded, w_kv_t[...], (((1,), (1,)), ((), ())), preferred_element_type=F32
    )
    for j in range(4):
        part_kv[:, 32 * j : 32 * j + 32] = new_kv[64 * j : 64 * j + 64]

    @pl.when(n != z)
    def _():
        to_hub_kv.start()

    for dx, part in LATE:
        exchange(dx, part)
    send_pages(1, CUT1)
    mine = query.at[y]
    seven_q = sum_q.at[pl.ds(0, 7)]
    seven_kv = sum_kv.at[pl.ds(0, 7)]

    @pl.when(n == z)
    def _():
        sum_q[pl.ds(n, 1)] = part_q[...][None]
        remote(seven_q, seven_q, s_b, r_b, (w, n)).wait_recv()
        query[pl.ds(y, 1)] = jnp.sum(sum_q[...].astype(F32), axis=0).astype(BF16)[None]

        def send_query(k, _):
            peer = ((z + k) % NZ) * NY + y
            remote(mine, mine, s_c2, r_c2, (peer, n)).start()
            return 0

        lax.fori_loop(1, NZ, send_query, 0)

    @pl.when(n != z)
    def _():
        remote(mine, mine, s_c2, r_c2, (w, n)).wait_recv()

    for dy in (1, 3, 2):
        remote(mine, mine, s_c3, r_c3, (z * NY + (y + dy) % NY, n)).start()

    @pl.when(n == z)
    def _():
        sum_kv[pl.ds(n, 1)] = part_kv[...][None]
        remote(seven_kv, seven_kv, s_bk, r_bk, (w, n)).wait_recv()
        kv_tiles[...] = jnp.sum(sum_kv[...], axis=0).astype(BF16).reshape(8, 8, HD)
        kv_four[pl.ds(y, 1)] = kv_tiles[...][None]

        def send_tile(k, _):
            peer = ((z + k) % NZ) * NY + y
            remote(kv_tiles, kv_four.at[y], s_k1, r_k1, (peer, n)).start()
            return 0

        lax.fori_loop(1, NZ, send_tile, 0)

    send_pages(CUT1, CUT2)

    def relay(dx, part):
        here = kv.at[2 * ((x + 4 - dx) % 4) + c, part]
        remote(here, here, s_x, r_x.at[dx - 1, part], (w, n)).wait_recv()
        remote(here, here, s_p, r_p.at[dx, part], (w, other)).start()

    for dx, part in EARLY:
        relay(dx, part)
    mine_kv = kv_four.at[y]

    @pl.when(n != z)
    def _():
        remote(mine_kv, mine_kv, s_k1, r_k1, (w, n)).wait_recv()

    for dy in (1, 3, 2):
        remote(mine_kv, mine_kv, s_k3, r_k3, (z * NY + (y + dy) % NY, n)).start()
    narrow_tiles = meta_n.at[pl.ds(0, NARROW - 1)]
    remote(narrow_tiles, narrow_tiles, s_mn, r_mn, (w, n)).wait()
    page_meta = meta_n[:, 1, :].astype(F32).astype(BF16)
    page = lax.broadcasted_iota(I32, (2 * POOL, POOL * PAGE), 0)
    page_of = lax.broadcasted_iota(I32, (2 * POOL, POOL * PAGE), 1) >> 4
    spread_req = (page == page_of).astype(F32).astype(BF16)
    spread_seen = (page - POOL == page_of).astype(F32).astype(BF16)
    owner = jnp.dot(page_meta, spread_req, preferred_element_type=F32)
    seen = jnp.dot(page_meta, spread_seen, preferred_element_type=F32)
    within = (lax.broadcasted_iota(I32, (NARROW, POOL * PAGE), 1) & 15).astype(F32)
    owner = jnp.where(within < seen, owner, -1.0)
    width = CHUNK * PAGE
    per = POOL // CHUNK
    for s in range(NARROW):
        for i in range(per):
            token_req[per * s + i] = jnp.broadcast_to(
                owner[s : s + 1, width * i : width * i + width], (8, width)
            )
    all_row = lax.broadcasted_iota(I32, (rows, 1), 0).astype(F32)
    row_req = jnp.floor((all_row + 0.5) * 0.2)
    row_req = jnp.concatenate([row_req] * 4, axis=0)
    three = query.at[pl.ds(0, 3)]
    spread_query = remote(three, three, s_c3, r_c3, (w, n))
    spread_query.wait_recv()

    for g, dx in enumerate(ORDER):
        from_other = kv.at[2 * ((x + 4 - dx) % 4) + (1 - c), 0]
        remote(from_other, from_other, s_p, r_p.at[dx, 0], (w, n)).wait_recv()

        def score(j, _, g=g, dx=dx):
            s = 2 * ((x + 4 - dx) % 4) + j // per
            i = j % per
            keys = kv[s, 0, pl.ds(i * CHUNK, CHUNK)].reshape(width, HD)
            raw = lax.dot_general(
                query[...].reshape(4 * rows, HD),
                keys,
                (((1,), (1,)), ((), ())),
                preferred_element_type=F32,
            )
            owners = token_req[per * s + i][0:1, :]
            raw = jnp.where(row_req == owners, raw, NEG)
            scores[2 * per * g + j] = raw
            top = raw[:, 0:HD]
            for t in range(1, width // HD):
                top = jnp.maximum(top, raw[:, HD * t : HD * t + HD])
            peaks[...] = jnp.maximum(peaks[...], top)
            return 0

        lax.fori_loop(0, 2 * per, score, 0)

    for dx, part in LATE:
        relay(dx, part)
    peak = jnp.max(peaks[...], axis=1, keepdims=True)
    ones = jnp.ones((width, HD), BF16)
    for g, dx in enumerate(ORDER):
        from_other = kv.at[2 * ((x + 4 - dx) % 4) + (1 - c), 1]
        remote(from_other, from_other, s_p, r_p.at[dx, 1], (w, n)).wait_recv()

        def weigh(j, _, g=g, dx=dx):
            s = 2 * ((x + 4 - dx) % 4) + j // per
            i = j % per
            values = kv[s, 1, pl.ds(i * CHUNK, CHUNK)].reshape(width, HD)
            weights = jnp.exp2(
                (scores[2 * per * g + j] - peak) * (SCALE * LOG2E)
            ).astype(BF16)
            acc[...] += jnp.dot(
                weights, jnp.concatenate([values, ones], axis=1), preferred_element_type=F32
            )
            return 0

        lax.fori_loop(0, 2 * per, weigh, 0)

    group = (lax.broadcasted_iota(I32, (rows, HD), 1) >> 3).astype(F32)
    srow = lax.broadcasted_iota(I32, (rows, HD), 0).astype(F32)
    step_of = srow - jnp.floor((srow + 0.5) * 0.2) * 5.0
    for h in range(4):
        here = slice(rows * h, rows * h + rows)
        terms = payload_stats(peak[here] * SCALE, acc[here, HD:], group, step_of)
        laid = jnp.dot(spread[0], acc[here, 0:HD].astype(BF16), preferred_element_type=F32)
        for k in range(3):
            laid += jnp.dot(spread[1 + k], terms[k], preferred_element_type=F32)
        partial[:, h] = laid.astype(BF16).reshape(WIDE, 8, HD)

    def send_partial(k, _):
        peer = (w + k) % WIDE
        remote(partial.at[peer], received.at[w], s_d, r_d, (peer, n)).start()
        return 0

    lax.fori_loop(1, WIDE, send_partial, 0)
    received[pl.ds(w, 1)] = partial[pl.ds(w, 1)]
    send_pages(CUT2, CUT3)

    lane = lax.broadcasted_iota(I32, (8, HD), 1)
    three_kv = kv_four.at[pl.ds(0, 3)]
    remote(three_kv, three_kv, s_k3, r_k3, (w, n)).wait()
    merged = jnp.zeros((8, HD), F32)
    for t in range(4):
        turned = pltpu.roll(kv_four[t, w % 8].astype(F32), (t + 4 - w // 8) % 4 * 32, 1)
        merged = merged + jnp.where((lane >= 32 * t) & (lane < 32 * t + 32), turned, 0.0)
    kv_new[pl.ds(n, 1)] = merged.astype(BF16)[None]

    def send_new(k, _):
        remote(kv_new.at[n], kv_new.at[n], s_k2, r_k2, (w, (n + k) % NARROW)).start()
        return 0

    lax.fori_loop(1, NARROW, send_new, 0)
    meta_lane = lax.broadcasted_iota(I32, (WIDE, HD), 1)
    slot_source = lax.broadcasted_iota(I32, (WIDE, POOL), 0)
    slot_lane = lax.broadcasted_iota(I32, (WIDE, POOL), 1)

    def arrived(line):
        values = hid_all[:, line : line + 1, 0:HD].astype(F32).reshape(WIDE, HD)
        result = jnp.zeros((1, POOL), F32)
        for k in range(2):
            column = jnp.sum(
                jnp.where(meta_lane == 2 * w + k, values, 0.0), axis=1, keepdims=True
            )
            result = result + jnp.sum(
                jnp.where(slot_lane == 2 * slot_source + k, column, 0.0), axis=0, keepdims=True
            )
        return result

    moved_req[...] = arrived(5).astype(I32)
    moved_idx[...] = (arrived(6) * 16.0 + arrived(7)).astype(I32)
    seven_new = kv_new.at[pl.ds(0, 7)]
    remote(seven_new, seven_new, s_k2, r_k2, (w, n)).wait()
    step = lax.broadcasted_iota(I32, (STEPS, HD), 0).astype(F32)
    for b in range(8):
        entries[0, :, HD * b : HD * b + HD] = jnp.where(
            step < accepted_here, kv_new[b][0:STEPS, :].astype(F32), 0.0
        ).astype(BF16)

    first_row = lax.broadcasted_iota(I32, (32, rows), 0)
    from_row = lax.broadcasted_iota(I32, (32, rows), 1)
    ours = (from_row == 5 * w + (first_row & 7)) & ((first_row & 7) < STEPS)
    ours = ours.astype(F32).astype(BF16)
    k_new = kv_new[x]
    v_new = kv_new[KVH + x]
    sub = lax.broadcasted_iota(I32, (8, HD), 0)
    lane_group = lane >> 3
    fresh_row = lax.broadcasted_iota(I32, (8, 8), 0)
    fresh_key = lax.broadcasted_iota(I32, (8, 8), 1)
    known = fresh_key <= fresh_row
    for h in range(4):
        q_new = jnp.dot(ours[0:8], query[h], preferred_element_type=F32).astype(BF16)
        fresh = lax.dot_general(
            q_new, k_new, (((1,), (1,)), ((), ())), preferred_element_type=F32
        ) * SCALE
        fresh = jnp.where(known, fresh, NEG)
        fresh_peak = jnp.max(fresh, axis=1, keepdims=True)
        fresh_weight = jnp.where(known, jnp.exp(fresh - fresh_peak), 0.0)
        fresh_total = jnp.sum(fresh_weight, axis=1, keepdims=True)
        fresh_sum = jnp.dot(fresh_weight.astype(BF16), v_new, preferred_element_type=F32)
        stat = jnp.where(
            lane_group == sub,
            fresh_peak,
            jnp.where(lane_group - 8 == sub, fresh_total, 0.0),
        )
        line = jnp.sum(jnp.where(sub < STEPS, stat, 0.0), axis=0, keepdims=True)
        first = line.astype(BF16).astype(F32)
        second = (line - first).astype(BF16).astype(F32)
        third = line - first - second
        tile = jnp.where(
            sub < STEPS,
            fresh_sum,
            jnp.where(sub == 5, first, jnp.where(sub == 6, second, third)),
        )
        received[WIDE, h] = tile.astype(BF16)

    others = received.at[pl.ds(0, WIDE - 1)]
    all_partial = remote(others, others, s_d, r_d, (w, n))
    all_partial.wait_recv()
    sub3 = lax.broadcasted_iota(I32, (1, 8, HD), 1)
    group3 = lax.broadcasted_iota(I32, (1, 8, HD), 2) >> 3
    for h in range(4):
        tiles = received[:, h].astype(F32)
        line = (tiles[:, 7:8] + tiles[:, 6:7]) + tiles[:, 5:6]
        high = jnp.max(jnp.where(group3 == sub3, line, -3e38), axis=2, keepdims=True)
        total = jnp.max(jnp.where(group3 - 8 == sub3, line, 0.0), axis=2, keepdims=True)
        top = jnp.max(high, axis=0, keepdims=True)
        factor = jnp.exp(high - top)
        total = jnp.sum(factor * total, axis=0)
        sums = jnp.sum(factor * tiles, axis=0)
        own[:, HD * h : HD * h + HD] = jnp.where(
            sub < STEPS, sums / jnp.where(sub < STEPS, total, 1.0), 0.0
        ).astype(BF16)
    gathered[pl.ds(w, 1)] = own[...][None]

    def send_own(k, _):
        remote(own, gathered.at[w], s_g, r_g, ((w + k) % WIDE, n)).start()
        return 0

    lax.fori_loop(1, WIDE, send_own, 0)
    send_pages(CUT3, 17)
    others = gathered.at[pl.ds(0, WIDE - 1)]
    all_rows = remote(others, others, s_g, r_g, (w, n))
    all_rows.wait_recv()
    loads[9].wait()
    attn = gathered[...].reshape(WIDE * 8, gathered.shape[2])
    product = jnp.dot(attn, w_out[...], preferred_element_type=F32)
    send_e[...] = product.astype(BF16).reshape(NARROW, 32, HD)
    recv_e[pl.ds(n, 1)] = send_e[pl.ds(n, 1)]

    def send_product(k, _):
        peer = (n + k) % NARROW
        remote(send_e.at[peer], recv_e.at[n], s_e, r_e, (w, peer)).start()
        return 0

    lax.fori_loop(1, NARROW, send_product, 0)
    others = recv_e.at[pl.ds(0, NARROW - 1)]
    all_products = remote(others, others, s_e, r_e, (w, n))
    all_products.wait_recv()
    result = jnp.sum(recv_e[...].astype(F32), axis=0)
    for j in range(4):
        attended[STEPS * j : STEPS * j + STEPS, :] = result[8 * j : 8 * j + STEPS].astype(BF16)

    all_hidden.wait_send()
    spread_query.wait_send()
    three = kv.at[pl.ds(0, 3)]
    remote(three, three, s_x, r_x.at[0, 0], (w, n)).wait_send()
    four = kv.at[pl.ds(0, 4)]
    remote(four, four, s_p, r_p.at[0, 0], (w, n)).wait_send()

    @pl.when(n != z)
    def _():
        to_hub_q.wait_send()
        to_hub_kv.wait_send()

    three_kv = kv_four.at[pl.ds(0, 3)]

    @pl.when(n == z)
    def _():
        remote(kv_four, kv_four, s_k1, r_k1, (w, n)).wait_send()
        remote(three_kv, three_kv, s_k1, r_k1, (w, n)).wait_send()
        four_q = query
        three_q = query.at[pl.ds(0, 3)]
        remote(four_q, four_q, s_c2, r_c2, (w, n)).wait_send()
        remote(three_q, three_q, s_c2, r_c2, (w, n)).wait_send()

    all_partial.wait_send()
    all_rows.wait_send()
    all_products.wait_send()
    stay.wait()
    gone = moved_out.at[pl.ds(0, POOL - 2)]
    remote(gone, gone, s_mig, r_mig, (w, n)).wait()


def deliver_kernel(*refs):
    sources, targets, (pages, sem_in, sem_out, sem_small) = refs[0:5], refs[5:10], refs[10:14]
    size = POOL // PIECES
    small = [
        pltpu.make_async_copy(sources[i], targets[i], sem_small.at[i]) for i in (0, 1, 3, 4)
    ]
    for copy in small:
        copy.start()
    parts = [pl.ds(size * i, size) for i in range(PIECES)]
    coming = [
        pltpu.make_async_copy(sources[2].at[part], pages.at[part], sem_in.at[i])
        for i, part in enumerate(parts)
    ]
    going = [
        pltpu.make_async_copy(pages.at[part], targets[2].at[part], sem_out.at[i])
        for i, part in enumerate(parts)
    ]
    for copy in coming:
        copy.start()
    for before, after in zip(coming, going):
        before.wait()
        after.start()
    for copy in going + small:
        copy.wait()


def on_device(hidden, w_query, w_keyval, w_out, pool, page_req, page_idx, lengths, moves, accepted):
    dma = pltpu.SemaphoreType.DMA
    shape = jax.ShapeDtypeStruct
    depth = hidden.shape[1]
    rows = WIDE * STEPS
    width = CHUNK * PAGE
    chunks = NARROW * POOL // CHUNK
    results = pl.pallas_call(
        whole_kernel,
        out_shape=(
            shape((4 * STEPS, HD), BF16),
            shape((1, STEPS, 1024), BF16),
            shape(pool.shape, BF16),
            shape((1, POOL), I32),
            shape((1, POOL), I32),
        ),
        in_specs=[ANY_SPEC] * 10,
        out_specs=(VMEM_SPEC, VMEM_SPEC, ANY_SPEC, VMEM_SPEC, VMEM_SPEC),
        scratch_shapes=[
            pltpu.VMEM((3, 1, POOL), I32),
            pltpu.VMEM((2, 1, WIDE), I32),
            pltpu.VMEM((STEPS, depth), BF16),
            pltpu.VMEM(w_query.shape, BF16),
            pltpu.VMEM(w_keyval.shape[::-1], BF16),
            pltpu.VMEM(w_out.shape, BF16),
            pltpu.VMEM((8, 128), I32),
            pltpu.VMEM((8, 128), I32),
            pltpu.SMEM((8, 128), I32),
            pltpu.VMEM((8, depth), BF16),
            pltpu.VMEM((WIDE, 8, depth), BF16),
            pltpu.VMEM((rows, HD), BF16),
            pltpu.VMEM((64, HD), F32),
            pltpu.VMEM((NARROW, rows, HD), BF16),
            pltpu.VMEM((NARROW, 64, HD), F32),
            pltpu.VMEM((4, rows, HD), BF16),
            pltpu.VMEM((8, 8, HD), BF16),
            pltpu.VMEM((4, 8, 8, HD), BF16),
            pltpu.VMEM((8, 8, HD), BF16),
            pltpu.VMEM((NARROW, 8, 128), I32),
            pltpu.VMEM(pool.shape, BF16),
            pltpu.VMEM(pool.shape, BF16),
            pltpu.VMEM((NARROW, 2, POOL, PAGE, HD), BF16),
            pltpu.VMEM((rows, WIDE * 8), BF16),
            pltpu.VMEM((4, WIDE * 8, rows), BF16),
            pltpu.VMEM((chunks, 8, width), F32),
            pltpu.VMEM((chunks, 4 * rows, width), F32),
            pltpu.VMEM((4 * rows, HD), F32),
            pltpu.VMEM((4 * rows, 2 * HD), F32),
            pltpu.VMEM((WIDE, 4, 8, HD), BF16),
            pltpu.VMEM((WIDE + 1, 4, 8, HD), BF16),
            pltpu.VMEM((8, 4 * HD), BF16),
            pltpu.VMEM((WIDE, 8, 4 * HD), BF16),
            pltpu.VMEM((NARROW, 32, HD), BF16),
            pltpu.VMEM((NARROW, 32, HD), BF16),
            dma((11,)), dma, dma, dma, dma, dma, dma,
            dma((5,)), dma, dma((3, 2)), dma, dma((4, 2)),
            dma, dma, dma, dma, dma, dma, dma, dma, dma, dma, dma, dma,
            dma, dma, dma, dma, dma, dma, dma, dma,
        ],
        compiler_params=pltpu.CompilerParams(
            collective_id=0, has_side_effects=True, vmem_limit_bytes=60 << 20
        ),
        name="verify_step",
    )(
        moves.reshape(1, POOL),
        page_req.reshape(1, POOL),
        page_idx.reshape(1, POOL),
        lengths.reshape(1, WIDE),
        accepted.reshape(1, WIDE),
        hidden,
        w_query,
        w_keyval.T,
        w_out,
        pool,
    )
    attended, entries, moved, moved_req, moved_idx = pl.pallas_call(
        deliver_kernel,
        out_shape=[shape(r.shape, r.dtype) for r in results],
        in_specs=[ANY_SPEC] * 5,
        out_specs=[ANY_SPEC] * 5,
        scratch_shapes=[
            pltpu.VMEM(pool.shape, BF16),
            dma((PIECES,)),
            dma((PIECES,)),
            dma((5,)),
        ],
        name="deliver",
    )(*results)
    return attended, entries, moved, moved_req.reshape(POOL), moved_idx.reshape(POOL)


def solution(mesh):
    in_specs = (
        P("wide", "narrow"),
        P("narrow", "wide"),
        P("narrow", "wide"),
        P("narrow", "wide"),
        P(("wide", "narrow"), None, None),
        P(("wide", "narrow")),
        P(("wide", "narrow")),
        P(),
        P(("wide", "narrow"), None),
        P(),
    )
    out_specs = (
        P("narrow", "wide"),
        P("wide", None, None),
        P(("wide", "narrow"), None, None),
        P(("wide", "narrow")),
        P(("wide", "narrow")),
    )
    return jax.shard_map(
        on_device, mesh=mesh, in_specs=in_specs, out_specs=out_specs, check_vma=False
    )
```

```python
import functools
import math

import jax
import jax.numpy as jnp
from jax import lax
from jax.experimental import pallas as pl
from jax.experimental.pallas import tpu as pltpu
from jax.sharding import PartitionSpec as P

HEADS = 32
KVH = 4
HD = 128
STEPS = 5
PAGE = 16
WIDE = 32
NARROW = 8
NY = 4
NZ = 8
POOL = 64
CHUNK = 32
PIECES = 4
EARLY = ((2, 0), (1, 0), (3, 0), (2, 1))
LATE = ((1, 1), (3, 1))
ORDER = (0, 2, 1, 3)
CUT0 = 6
CUT1 = 8
CUT2 = 14
CUT3 = 15
SCALE = 1.0 / math.sqrt(HD)
LOG2E = 1.4426950408889634
NEG = -1e30
F32 = jnp.float32
BF16 = jnp.bfloat16
I32 = jnp.int32
MESH = pl.DeviceIdType.MESH
VMEM_SPEC = pl.BlockSpec(memory_space=pltpu.VMEM)
SMEM_SPEC = pl.BlockSpec(memory_space=pltpu.SMEM)
ANY_SPEC = pl.BlockSpec(memory_space=pl.ANY)


def greet(w, n, barrier):

    def wide_signal(k, _):
        pl.semaphore_signal(
            barrier, inc=1, device_id=((w + k) % WIDE, n), device_id_type=MESH
        )
        return 0

    def narrow_signal(k, _):
        pl.semaphore_signal(
            barrier, inc=1, device_id=(w, (n + k) % NARROW), device_id_type=MESH
        )
        return 0

    lax.fori_loop(1, WIDE, wide_signal, 0)
    lax.fori_loop(1, NARROW, narrow_signal, 0)


def remote(src, dst, send, recv, device):
    return pltpu.make_async_remote_copy(
        src_ref=src,
        dst_ref=dst,
        send_sem=send,
        recv_sem=recv,
        device_id=device,
        device_id_type=MESH,
    )


def payload_stats(peak, total, group, step):
    stat = jnp.where(group == step, peak, jnp.where(group - 8 == step, total, 0.0))
    first = stat.astype(BF16)
    rest = stat - first.astype(F32)
    second = rest.astype(BF16)
    third = (rest - second.astype(F32)).astype(BF16)
    return first, second, third


def whole_kernel(
    moves, page_req, page_idx, lengths, accepted, hidden, w_query_in, w_kv_in, w_out_in, pool,
    attended, entries, moved_out, moved_req, moved_idx,
    small, small_len, hid_in, w_query, w_kv_t, w_out, meta, source_v, source,
    hid_own, hid_all, part_q, part_kv, sum_q, sum_kv, query, kv_tiles, kv_four, kv_new,
    meta_n, pool_v, leaving, kv, pick, spread,
    token_req, scores, peaks, acc, partial, received, own, gathered, send_e, recv_e,
    l_in, s_a, r_a, s_mn, r_mn, s_mig, r_mig, l_sem, s_x, r_x, s_p, r_p,
    s_b, r_b, s_bk, r_bk, s_k1, r_k1, s_k3, r_k3, s_c2, r_c2, s_k2, r_k2, s_c3, r_c3,
    s_d, r_d, s_g, r_g, s_e, r_e,
):
    w = lax.axis_index("wide")
    n = lax.axis_index("narrow")
    z = w // NY
    y = w % NY
    x = n // 2
    c = n % 2
    other = 2 * x + (1 - c)
    rows = WIDE * STEPS
    loads = []
    for i, (origin, target) in enumerate(
        (
            (moves, small.at[0]),
            (page_req, small.at[1]),
            (page_idx, small.at[2]),
            (lengths, small_len.at[0]),
            (accepted, small_len.at[1]),
            (hidden, hid_in),
            (pool, pool_v),
            (w_query_in, w_query),
            (w_kv_in, w_kv_t),
            (w_out_in, w_out),
        )
    ):
        loads.append(pltpu.make_async_copy(origin, target, l_in.at[i]))
        loads[-1].start()
    barrier = pltpu.get_barrier_semaphore()
    greet(w, n, barrier)
    for load in loads[0:6]:
        load.wait()
    hid_own[...] = jnp.zeros_like(hid_own)
    hid_own[0:STEPS, :] = hid_in[...]
    sub64 = lax.broadcasted_iota(I32, (POOL, POOL), 0).astype(F32)
    lane64 = lax.broadcasted_iota(I32, (POOL, POOL), 1).astype(F32)
    diagonal = sub64 == lane64

    def as_column(line):
        return jnp.sum(jnp.where(diagonal, line, 0.0), axis=1, keepdims=True)

    leave = small[0].astype(F32)
    leave_column = as_column(leave)
    earlier = (leave_column == leave) & (lane64 < sub64)
    rank = jnp.sum(earlier.astype(F32), axis=1, keepdims=True)
    taken = leave_column * 2.0 + rank == lane64
    req_line = small[1].astype(F32)
    idx_line = small[2].astype(F32)

    def reorder(line):
        return jnp.sum(jnp.where(taken, as_column(line), 0.0), axis=0, keepdims=True)

    source_row = jnp.sum(jnp.where(taken, sub64, 0.0), axis=0, keepdims=True).astype(I32)
    source_v[...] = jnp.zeros_like(source_v)
    source_v[0:1, 0:POOL] = source_row
    sub32 = lax.broadcasted_iota(I32, (WIDE, WIDE), 0)
    lane32 = lax.broadcasted_iota(I32, (WIDE, WIDE), 1)
    len_column = jnp.sum(
        jnp.where(sub32 == lane32, small_len[0].astype(F32), 0.0), axis=1, keepdims=True
    )
    owner_is = lax.broadcasted_iota(I32, (WIDE, POOL), 0).astype(F32) == req_line
    length_of = jnp.sum(jnp.where(owner_is, len_column, 0.0), axis=0, keepdims=True)
    seen_line = jnp.clip(length_of - idx_line * PAGE, 0.0, float(PAGE))
    seen_line = jnp.where(req_line >= 0.0, seen_line, 0.0)
    meta[...] = jnp.zeros_like(meta)
    idx_high = jnp.floor(idx_line * (1.0 / 16.0))
    hid_own[5:6, 0:POOL] = reorder(req_line).astype(BF16)
    hid_own[6:7, 0:POOL] = reorder(idx_high).astype(BF16)
    hid_own[7:8, 0:POOL] = reorder(idx_line - idx_high * 16.0).astype(BF16)
    meta[1:2, 0:POOL] = req_line.astype(I32)
    meta[1:2, POOL : 2 * POOL] = seen_line.astype(I32)
    lane_w = lax.broadcasted_iota(I32, (1, WIDE), 1)
    accepted_here = jnp.sum(
        jnp.where(lane_w == w, small_len[1].astype(F32), 0.0), axis=1, keepdims=True
    )
    to_scalar = pltpu.make_async_copy(source_v, source, l_in.at[10])
    to_scalar.start()
    hid_all[pl.ds(w, 1)] = hid_own[...][None]
    meta_n[pl.ds(n, 1)] = meta[...][None]
    pl.semaphore_wait(barrier, WIDE + NARROW - 2)

    def block_of(part, head):
        return pl.ds(pl.multiple_of(KVH * HD * part + HD * head, HD), HD)

    def exchange(dx, part):
        tx = (x + dx) % 4
        remote(
            pool.at[:, :, block_of(part, tx)],
            kv.at[n, part],
            s_x,
            r_x.at[dx - 1, part],
            (w, 2 * tx + c),
        ).start()

    for dx, part in EARLY:
        exchange(dx, part)

    def send_hidden(k, _):
        remote(hid_own, hid_all.at[w], s_a, r_a, ((w + k) % WIDE, n)).start()
        return 0

    lax.fori_loop(1, WIDE, send_hidden, 0)

    def send_meta_narrow(k, _):
        remote(meta, meta_n.at[n], s_mn, r_mn, (w, (n + k) % NARROW)).start()
        return 0

    lax.fori_loop(1, NARROW, send_meta_narrow, 0)

    for part in range(2):
        mine_here = pool.at[:, :, block_of(part, x)]
        remote(mine_here, kv.at[n, part], s_p, r_p.at[0, part], (w, other)).start()
    row = lax.broadcasted_iota(I32, (rows, WIDE * 8), 0).astype(F32)
    col = lax.broadcasted_iota(I32, (rows, WIDE * 8), 1).astype(F32)
    req_of_row = jnp.floor((row + 0.5) * 0.2)
    pick[...] = (col == req_of_row * 3.0 + row).astype(F32).astype(BF16)
    slot = lax.broadcasted_iota(I32, (WIDE * 8, rows), 0)
    req_of_slot = (slot >> 3).astype(F32)
    place = (slot & 7).astype(F32)
    origin = lax.broadcasted_iota(I32, (WIDE * 8, rows), 1).astype(F32)
    req_of_origin = jnp.floor((origin + 0.5) * 0.2)
    step_of_origin = origin - req_of_origin * 5.0
    same = req_of_slot == req_of_origin
    spread[0] = (same & (place == step_of_origin)).astype(F32).astype(BF16)
    for k in range(3):
        spread[1 + k] = (same & (place == 5.0 + k)).astype(F32).astype(BF16)
    peaks[...] = jnp.full(peaks.shape, NEG, F32)
    acc[...] = jnp.zeros_like(acc)

    to_scalar.wait()
    loads[6].wait()

    def take_page(j, _):
        leaving[j] = pool_v[jnp.clip(source[0, j], 0, POOL - 1)]
        for part in range(2):
            kv[n, part, j] = pool_v[j, :, block_of(part, x)]
        return 0

    lax.fori_loop(0, POOL, take_page, 0)
    stay = pltpu.make_async_copy(
        leaving.at[pl.ds(2 * w, 2)], moved_out.at[pl.ds(2 * w, 2)], l_sem.at[3]
    )
    stay.start()

    def send_pages(first, last):
        def send_pair(i, _):
            for k in (i, WIDE - i):
                peer = (w + k) % WIDE
                remote(
                    leaving.at[pl.ds(2 * peer, 2)],
                    moved_out.at[pl.ds(2 * w, 2)],
                    s_mig,
                    r_mig,
                    (peer, n),
                ).start()
            return 0

        lax.fori_loop(first, min(last, 16), send_pair, 0)
        if first <= 16 < last:
            peer = (w + 16) % WIDE
            remote(
                leaving.at[pl.ds(2 * peer, 2)],
                moved_out.at[pl.ds(2 * w, 2)],
                s_mig,
                r_mig,
                (peer, n),
            ).start()

    send_pages(1, CUT0)
    others = hid_all.at[pl.ds(0, WIDE - 1)]
    all_hidden = remote(others, others, s_a, r_a, (w, n))
    all_hidden.wait_recv()
    padded = hid_all[...].reshape(WIDE * 8, hid_all.shape[2])
    loads[7].wait()
    loads[8].wait()
    packed = jnp.dot(pick[...], padded, preferred_element_type=F32).astype(BF16)
    part_q[...] = jnp.dot(packed, w_query[...], preferred_element_type=F32).astype(BF16)
    to_hub_q = remote(part_q, sum_q.at[n], s_b, r_b, (w, z))
    to_hub_kv = remote(part_kv, sum_kv.at[n], s_bk, r_bk, (w, z))

    @pl.when(n != z)
    def _():
        to_hub_q.start()

    new_kv = lax.dot_general(
        padded, w_kv_t[...], (((1,), (1,)), ((), ())), preferred_element_type=F32
    )
    for j in range(4):
        part_kv[:, 32 * j : 32 * j + 32] = new_kv[64 * j : 64 * j + 64]

    @pl.when(n != z)
    def _():
        to_hub_kv.start()

    for dx, part in LATE:
        exchange(dx, part)
    send_pages(CUT0, CUT1)
    mine = query.at[y]
    seven_q = sum_q.at[pl.ds(0, 7)]
    seven_kv = sum_kv.at[pl.ds(0, 7)]

    @pl.when(n == z)
    def _():
        sum_q[pl.ds(n, 1)] = part_q[...][None]
        remote(seven_q, seven_q, s_b, r_b, (w, n)).wait_recv()
        query[pl.ds(y, 1)] = jnp.sum(sum_q[...].astype(F32), axis=0).astype(BF16)[None]

        def send_query(k, _):
            peer = ((z + k) % NZ) * NY + y
            remote(mine, mine, s_c2, r_c2, (peer, n)).start()
            return 0

        lax.fori_loop(1, NZ, send_query, 0)

    @pl.when(n != z)
    def _():
        remote(mine, mine, s_c2, r_c2, (w, n)).wait_recv()

    for dy in (1, 3, 2):
        remote(mine, mine, s_c3, r_c3, (z * NY + (y + dy) % NY, n)).start()

    @pl.when(n == z)
    def _():
        sum_kv[pl.ds(n, 1)] = part_kv[...][None]
        remote(seven_kv, seven_kv, s_bk, r_bk, (w, n)).wait_recv()
        kv_tiles[...] = jnp.sum(sum_kv[...], axis=0).astype(BF16).reshape(8, 8, HD)
        kv_four[pl.ds(y, 1)] = kv_tiles[...][None]

        def send_tile(k, _):
            peer = ((z + k) % NZ) * NY + y
            remote(kv_tiles, kv_four.at[y], s_k1, r_k1, (peer, n)).start()
            return 0

        lax.fori_loop(1, NZ, send_tile, 0)

    send_pages(CUT1, CUT2)

    def relay(dx, part):
        here = kv.at[2 * ((x + 4 - dx) % 4) + c, part]
        remote(here, here, s_x, r_x.at[dx - 1, part], (w, n)).wait_recv()
        remote(here, here, s_p, r_p.at[dx, part], (w, other)).start()

    for dx, part in EARLY:
        relay(dx, part)
    mine_kv = kv_four.at[y]

    @pl.when(n != z)
    def _():
        remote(mine_kv, mine_kv, s_k1, r_k1, (w, n)).wait_recv()

    for dy in (1, 3, 2):
        remote(mine_kv, mine_kv, s_k3, r_k3, (z * NY + (y + dy) % NY, n)).start()
    narrow_tiles = meta_n.at[pl.ds(0, NARROW - 1)]
    remote(narrow_tiles, narrow_tiles, s_mn, r_mn, (w, n)).wait()
    page_meta = meta_n[:, 1, :].astype(F32).astype(BF16)
    page = lax.broadcasted_iota(I32, (2 * POOL, POOL * PAGE), 0)
    page_of = lax.broadcasted_iota(I32, (2 * POOL, POOL * PAGE), 1) >> 4
    spread_req = (page == page_of).astype(F32).astype(BF16)
    spread_seen = (page - POOL == page_of).astype(F32).astype(BF16)
    owner = jnp.dot(page_meta, spread_req, preferred_element_type=F32)
    seen = jnp.dot(page_meta, spread_seen, preferred_element_type=F32)
    within = (lax.broadcasted_iota(I32, (NARROW, POOL * PAGE), 1) & 15).astype(F32)
    owner = jnp.where(within < seen, owner, -1.0)
    width = CHUNK * PAGE
    per = POOL // CHUNK
    for s in range(NARROW):
        for i in range(per):
            token_req[per * s + i] = jnp.broadcast_to(
                owner[s : s + 1, width * i : width * i + width], (8, width)
            )
    all_row = lax.broadcasted_iota(I32, (rows, 1), 0).astype(F32)
    row_req = jnp.floor((all_row + 0.5) * 0.2)
    row_req = jnp.concatenate([row_req] * 4, axis=0)
    three = query.at[pl.ds(0, 3)]
    spread_query = remote(three, three, s_c3, r_c3, (w, n))
    spread_query.wait_recv()

    for g, dx in enumerate(ORDER):
        from_other = kv.at[2 * ((x + 4 - dx) % 4) + (1 - c), 0]
        remote(from_other, from_other, s_p, r_p.at[dx, 0], (w, n)).wait_recv()

        def score(j, _, g=g, dx=dx):
            s = 2 * ((x + 4 - dx) % 4) + j // per
            i = j % per
            keys = kv[s, 0, pl.ds(i * CHUNK, CHUNK)].reshape(width, HD)
            raw = lax.dot_general(
                query[...].reshape(4 * rows, HD),
                keys,
                (((1,), (1,)), ((), ())),
                preferred_element_type=F32,
            )
            owners = token_req[per * s + i][0:1, :]
            raw = jnp.where(row_req == owners, raw, NEG)
            scores[2 * per * g + j] = raw
            top = raw[:, 0:HD]
            for t in range(1, width // HD):
                top = jnp.maximum(top, raw[:, HD * t : HD * t + HD])
            peaks[...] = jnp.maximum(peaks[...], top)
            return 0

        lax.fori_loop(0, 2 * per, score, 0)

    for dx, part in LATE:
        relay(dx, part)
    peak = jnp.max(peaks[...], axis=1, keepdims=True)
    ones = jnp.ones((width, HD), BF16)
    for g, dx in enumerate(ORDER):
        from_other = kv.at[2 * ((x + 4 - dx) % 4) + (1 - c), 1]
        remote(from_other, from_other, s_p, r_p.at[dx, 1], (w, n)).wait_recv()

        def weigh(j, _, g=g, dx=dx):
            s = 2 * ((x + 4 - dx) % 4) + j // per
            i = j % per
            values = kv[s, 1, pl.ds(i * CHUNK, CHUNK)].reshape(width, HD)
            weights = jnp.exp2(
                (scores[2 * per * g + j] - peak) * (SCALE * LOG2E)
            ).astype(BF16)
            acc[...] += jnp.dot(
                weights, jnp.concatenate([values, ones], axis=1), preferred_element_type=F32
            )
            return 0

        lax.fori_loop(0, 2 * per, weigh, 0)

    group = (lax.broadcasted_iota(I32, (rows, HD), 1) >> 3).astype(F32)
    srow = lax.broadcasted_iota(I32, (rows, HD), 0).astype(F32)
    step_of = srow - jnp.floor((srow + 0.5) * 0.2) * 5.0
    for h in range(4):
        here = slice(rows * h, rows * h + rows)
        terms = payload_stats(peak[here] * SCALE, acc[here, HD:], group, step_of)
        laid = jnp.dot(spread[0], acc[here, 0:HD].astype(BF16), preferred_element_type=F32)
        for k in range(3):
            laid += jnp.dot(spread[1 + k], terms[k], preferred_element_type=F32)
        partial[:, h] = laid.astype(BF16).reshape(WIDE, 8, HD)

    def send_partial(k, _):
        peer = (w + k) % WIDE
        remote(partial.at[peer], received.at[w], s_d, r_d, (peer, n)).start()
        return 0

    lax.fori_loop(1, WIDE, send_partial, 0)
    received[pl.ds(w, 1)] = partial[pl.ds(w, 1)]
    send_pages(CUT2, CUT3)

    lane = lax.broadcasted_iota(I32, (8, HD), 1)
    three_kv = kv_four.at[pl.ds(0, 3)]
    remote(three_kv, three_kv, s_k3, r_k3, (w, n)).wait()
    merged = jnp.zeros((8, HD), F32)
    for t in range(4):
        turned = pltpu.roll(kv_four[t, w % 8].astype(F32), (t + 4 - w // 8) % 4 * 32, 1)
        merged = merged + jnp.where((lane >= 32 * t) & (lane < 32 * t + 32), turned, 0.0)
    kv_new[pl.ds(n, 1)] = merged.astype(BF16)[None]

    def send_new(k, _):
        remote(kv_new.at[n], kv_new.at[n], s_k2, r_k2, (w, (n + k) % NARROW)).start()
        return 0

    lax.fori_loop(1, NARROW, send_new, 0)
    meta_lane = lax.broadcasted_iota(I32, (WIDE, HD), 1)
    slot_source = lax.broadcasted_iota(I32, (WIDE, POOL), 0)
    slot_lane = lax.broadcasted_iota(I32, (WIDE, POOL), 1)

    def arrived(line):
        values = hid_all[:, line : line + 1, 0:HD].astype(F32).reshape(WIDE, HD)
        result = jnp.zeros((1, POOL), F32)
        for k in range(2):
            column = jnp.sum(
                jnp.where(meta_lane == 2 * w + k, values, 0.0), axis=1, keepdims=True
            )
            result = result + jnp.sum(
                jnp.where(slot_lane == 2 * slot_source + k, column, 0.0), axis=0, keepdims=True
            )
        return result

    moved_req[...] = arrived(5).astype(I32)
    moved_idx[...] = (arrived(6) * 16.0 + arrived(7)).astype(I32)
    seven_new = kv_new.at[pl.ds(0, 7)]
    remote(seven_new, seven_new, s_k2, r_k2, (w, n)).wait()
    step = lax.broadcasted_iota(I32, (STEPS, HD), 0).astype(F32)
    for b in range(8):
        entries[0, :, HD * b : HD * b + HD] = jnp.where(
            step < accepted_here, kv_new[b][0:STEPS, :].astype(F32), 0.0
        ).astype(BF16)

    first_row = lax.broadcasted_iota(I32, (32, rows), 0)
    from_row = lax.broadcasted_iota(I32, (32, rows), 1)
    ours = (from_row == 5 * w + (first_row & 7)) & ((first_row & 7) < STEPS)
    ours = ours.astype(F32).astype(BF16)
    k_new = kv_new[x]
    v_new = kv_new[KVH + x]
    sub = lax.broadcasted_iota(I32, (8, HD), 0)
    lane_group = lane >> 3
    fresh_row = lax.broadcasted_iota(I32, (8, 8), 0)
    fresh_key = lax.broadcasted_iota(I32, (8, 8), 1)
    known = fresh_key <= fresh_row
    for h in range(4):
        q_new = jnp.dot(ours[0:8], query[h], preferred_element_type=F32).astype(BF16)
        fresh = lax.dot_general(
            q_new, k_new, (((1,), (1,)), ((), ())), preferred_element_type=F32
        ) * SCALE
        fresh = jnp.where(known, fresh, NEG)
        fresh_peak = jnp.max(fresh, axis=1, keepdims=True)
        fresh_weight = jnp.where(known, jnp.exp(fresh - fresh_peak), 0.0)
        fresh_total = jnp.sum(fresh_weight, axis=1, keepdims=True)
        fresh_sum = jnp.dot(fresh_weight.astype(BF16), v_new, preferred_element_type=F32)
        stat = jnp.where(
            lane_group == sub,
            fresh_peak,
            jnp.where(lane_group - 8 == sub, fresh_total, 0.0),
        )
        line = jnp.sum(jnp.where(sub < STEPS, stat, 0.0), axis=0, keepdims=True)
        first = line.astype(BF16).astype(F32)
        second = (line - first).astype(BF16).astype(F32)
        third = line - first - second
        tile = jnp.where(
            sub < STEPS,
            fresh_sum,
            jnp.where(sub == 5, first, jnp.where(sub == 6, second, third)),
        )
        received[WIDE, h] = tile.astype(BF16)

    others = received.at[pl.ds(0, WIDE - 1)]
    all_partial = remote(others, others, s_d, r_d, (w, n))
    all_partial.wait_recv()
    sub3 = lax.broadcasted_iota(I32, (1, 8, HD), 1)
    group3 = lax.broadcasted_iota(I32, (1, 8, HD), 2) >> 3
    for h in range(4):
        tiles = received[:, h].astype(F32)
        line = (tiles[:, 7:8] + tiles[:, 6:7]) + tiles[:, 5:6]
        high = jnp.max(jnp.where(group3 == sub3, line, -3e38), axis=2, keepdims=True)
        total = jnp.max(jnp.where(group3 - 8 == sub3, line, 0.0), axis=2, keepdims=True)
        top = jnp.max(high, axis=0, keepdims=True)
        factor = jnp.exp(high - top)
        total = jnp.sum(factor * total, axis=0)
        sums = jnp.sum(factor * tiles, axis=0)
        own[:, HD * h : HD * h + HD] = jnp.where(
            sub < STEPS, sums / jnp.where(sub < STEPS, total, 1.0), 0.0
        ).astype(BF16)
    gathered[pl.ds(w, 1)] = own[...][None]

    def send_own(k, _):
        remote(own, gathered.at[w], s_g, r_g, ((w + k) % WIDE, n)).start()
        return 0

    lax.fori_loop(1, WIDE, send_own, 0)
    send_pages(CUT3, 17)
    others = gathered.at[pl.ds(0, WIDE - 1)]
    all_rows = remote(others, others, s_g, r_g, (w, n))
    all_rows.wait_recv()
    loads[9].wait()
    attn = gathered[...].reshape(WIDE * 8, gathered.shape[2])
    product = jnp.dot(attn, w_out[...], preferred_element_type=F32)
    send_e[...] = product.astype(BF16).reshape(NARROW, 32, HD)
    recv_e[pl.ds(n, 1)] = send_e[pl.ds(n, 1)]

    def send_product(k, _):
        peer = (n + k) % NARROW
        remote(send_e.at[peer], recv_e.at[n], s_e, r_e, (w, peer)).start()
        return 0

    lax.fori_loop(1, NARROW, send_product, 0)
    others = recv_e.at[pl.ds(0, NARROW - 1)]
    all_products = remote(others, others, s_e, r_e, (w, n))
    all_products.wait_recv()
    result = jnp.sum(recv_e[...].astype(F32), axis=0)
    for j in range(4):
        attended[STEPS * j : STEPS * j + STEPS, :] = result[8 * j : 8 * j + STEPS].astype(BF16)

    all_hidden.wait_send()
    spread_query.wait_send()
    three = kv.at[pl.ds(0, 3)]
    remote(three, three, s_x, r_x.at[0, 0], (w, n)).wait_send()
    four = kv.at[pl.ds(0, 4)]
    remote(four, four, s_p, r_p.at[0, 0], (w, n)).wait_send()

    @pl.when(n != z)
    def _():
        to_hub_q.wait_send()
        to_hub_kv.wait_send()

    three_kv = kv_four.at[pl.ds(0, 3)]

    @pl.when(n == z)
    def _():
        remote(kv_four, kv_four, s_k1, r_k1, (w, n)).wait_send()
        remote(three_kv, three_kv, s_k1, r_k1, (w, n)).wait_send()
        four_q = query
        three_q = query.at[pl.ds(0, 3)]
        remote(four_q, four_q, s_c2, r_c2, (w, n)).wait_send()
        remote(three_q, three_q, s_c2, r_c2, (w, n)).wait_send()

    all_partial.wait_send()
    all_rows.wait_send()
    all_products.wait_send()
    stay.wait()
    gone = moved_out.at[pl.ds(0, POOL - 2)]
    remote(gone, gone, s_mig, r_mig, (w, n)).wait()


def deliver_kernel(*refs):
    sources, targets, (pages, sem_in, sem_out, sem_small) = refs[0:5], refs[5:10], refs[10:14]
    size = POOL // PIECES
    small = [
        pltpu.make_async_copy(sources[i], targets[i], sem_small.at[i]) for i in (0, 1, 3, 4)
    ]
    for copy in small:
        copy.start()
    parts = [pl.ds(size * i, size) for i in range(PIECES)]
    coming = [
        pltpu.make_async_copy(sources[2].at[part], pages.at[part], sem_in.at[i])
        for i, part in enumerate(parts)
    ]
    going = [
        pltpu.make_async_copy(pages.at[part], targets[2].at[part], sem_out.at[i])
        for i, part in enumerate(parts)
    ]
    for copy in coming:
        copy.start()
    for before, after in zip(coming, going):
        before.wait()
        after.start()
    for copy in going + small:
        copy.wait()


def on_device(hidden, w_query, w_keyval, w_out, pool, page_req, page_idx, lengths, moves, accepted):
    dma = pltpu.SemaphoreType.DMA
    shape = jax.ShapeDtypeStruct
    depth = hidden.shape[1]
    rows = WIDE * STEPS
    width = CHUNK * PAGE
    chunks = NARROW * POOL // CHUNK
    results = pl.pallas_call(
        whole_kernel,
        out_shape=(
            shape((4 * STEPS, HD), BF16),
            shape((1, STEPS, 1024), BF16),
            shape(pool.shape, BF16),
            shape((1, POOL), I32),
            shape((1, POOL), I32),
        ),
        in_specs=[ANY_SPEC] * 10,
        out_specs=(VMEM_SPEC, VMEM_SPEC, ANY_SPEC, VMEM_SPEC, VMEM_SPEC),
        scratch_shapes=[
            pltpu.VMEM((3, 1, POOL), I32),
            pltpu.VMEM((2, 1, WIDE), I32),
            pltpu.VMEM((STEPS, depth), BF16),
            pltpu.VMEM(w_query.shape, BF16),
            pltpu.VMEM(w_keyval.shape[::-1], BF16),
            pltpu.VMEM(w_out.shape, BF16),
            pltpu.VMEM((8, 128), I32),
            pltpu.VMEM((8, 128), I32),
            pltpu.SMEM((8, 128), I32),
            pltpu.VMEM((8, depth), BF16),
            pltpu.VMEM((WIDE, 8, depth), BF16),
            pltpu.VMEM((rows, HD), BF16),
            pltpu.VMEM((64, HD), F32),
            pltpu.VMEM((NARROW, rows, HD), BF16),
            pltpu.VMEM((NARROW, 64, HD), F32),
            pltpu.VMEM((4, rows, HD), BF16),
            pltpu.VMEM((8, 8, HD), BF16),
            pltpu.VMEM((4, 8, 8, HD), BF16),
            pltpu.VMEM((8, 8, HD), BF16),
            pltpu.VMEM((NARROW, 8, 128), I32),
            pltpu.VMEM(pool.shape, BF16),
            pltpu.VMEM(pool.shape, BF16),
            pltpu.VMEM((NARROW, 2, POOL, PAGE, HD), BF16),
            pltpu.VMEM((rows, WIDE * 8), BF16),
            pltpu.VMEM((4, WIDE * 8, rows), BF16),
            pltpu.VMEM((chunks, 8, width), F32),
            pltpu.VMEM((chunks, 4 * rows, width), F32),
            pltpu.VMEM((4 * rows, HD), F32),
            pltpu.VMEM((4 * rows, 2 * HD), F32),
            pltpu.VMEM((WIDE, 4, 8, HD), BF16),
            pltpu.VMEM((WIDE + 1, 4, 8, HD), BF16),
            pltpu.VMEM((8, 4 * HD), BF16),
            pltpu.VMEM((WIDE, 8, 4 * HD), BF16),
            pltpu.VMEM((NARROW, 32, HD), BF16),
            pltpu.VMEM((NARROW, 32, HD), BF16),
            dma((11,)), dma, dma, dma, dma, dma, dma,
            dma((5,)), dma, dma((3, 2)), dma, dma((4, 2)),
            dma, dma, dma, dma, dma, dma, dma, dma, dma, dma, dma, dma,
            dma, dma, dma, dma, dma, dma, dma, dma,
        ],
        compiler_params=pltpu.CompilerParams(
            collective_id=0, has_side_effects=True, vmem_limit_bytes=60 << 20
        ),
        name="verify_step",
    )(
        moves.reshape(1, POOL),
        page_req.reshape(1, POOL),
        page_idx.reshape(1, POOL),
        lengths.reshape(1, WIDE),
        accepted.reshape(1, WIDE),
        hidden,
        w_query,
        w_keyval.T,
        w_out,
        pool,
    )
    attended, entries, moved, moved_req, moved_idx = pl.pallas_call(
        deliver_kernel,
        out_shape=[shape(r.shape, r.dtype) for r in results],
        in_specs=[ANY_SPEC] * 5,
        out_specs=[ANY_SPEC] * 5,
        scratch_shapes=[
            pltpu.VMEM(pool.shape, BF16),
            dma((PIECES,)),
            dma((PIECES,)),
            dma((5,)),
        ],
        name="deliver",
    )(*results)
    return attended, entries, moved, moved_req.reshape(POOL), moved_idx.reshape(POOL)


def solution(mesh):
    in_specs = (
        P("wide", "narrow"),
        P("narrow", "wide"),
        P("narrow", "wide"),
        P("narrow", "wide"),
        P(("wide", "narrow"), None, None),
        P(("wide", "narrow")),
        P(("wide", "narrow")),
        P(),
        P(("wide", "narrow"), None),
        P(),
    )
    out_specs = (
        P("narrow", "wide"),
        P("wide", None, None),
        P(("wide", "narrow"), None, None),
        P(("wide", "narrow")),
        P(("wide", "narrow")),
    )
    return jax.shard_map(
        on_device, mesh=mesh, in_specs=in_specs, out_specs=out_specs, check_vma=False
    )
```

```python
import functools
import math

import jax
import jax.numpy as jnp
from jax import lax
from jax.experimental import pallas as pl
from jax.experimental.pallas import tpu as pltpu
from jax.sharding import PartitionSpec as P

HEADS = 32
KVH = 4
HD = 128
STEPS = 5
PAGE = 16
WIDE = 32
NARROW = 8
NY = 4
NZ = 8
POOL = 64
CHUNK = 32
PIECES = 4
EARLY = ((2, 0), (1, 0), (3, 0), (2, 1))
LATE = ((1, 1), (3, 1))
ORDER = (0, 2, 1, 3)
CUT0 = 6
CUT1 = 8
CUT2 = 14
CUT3 = 15
SCALE = 1.0 / math.sqrt(HD)
LOG2E = 1.4426950408889634
NEG = -1e30
F32 = jnp.float32
BF16 = jnp.bfloat16
I32 = jnp.int32
MESH = pl.DeviceIdType.MESH
VMEM_SPEC = pl.BlockSpec(memory_space=pltpu.VMEM)
SMEM_SPEC = pl.BlockSpec(memory_space=pltpu.SMEM)
ANY_SPEC = pl.BlockSpec(memory_space=pl.ANY)


def greet(w, n, barrier):

    def wide_signal(k, _):
        pl.semaphore_signal(
            barrier, inc=1, device_id=((w + k) % WIDE, n), device_id_type=MESH
        )
        return 0

    def narrow_signal(k, _):
        pl.semaphore_signal(
            barrier, inc=1, device_id=(w, (n + k) % NARROW), device_id_type=MESH
        )
        return 0

    lax.fori_loop(1, WIDE, wide_signal, 0)
    lax.fori_loop(1, NARROW, narrow_signal, 0)


def remote(src, dst, send, recv, device):
    return pltpu.make_async_remote_copy(
        src_ref=src,
        dst_ref=dst,
        send_sem=send,
        recv_sem=recv,
        device_id=device,
        device_id_type=MESH,
    )


def payload_stats(peak, total, group, step):
    stat = jnp.where(group == step, peak, jnp.where(group - 8 == step, total, 0.0))
    first = stat.astype(BF16)
    rest = stat - first.astype(F32)
    second = rest.astype(BF16)
    third = (rest - second.astype(F32)).astype(BF16)
    return first, second, third


def whole_kernel(
    moves, page_req, page_idx, lengths, accepted, hidden, w_query_in, w_kv_in, w_out_in, pool,
    attended, entries, moved_out, moved_req, moved_idx,
    small, small_len, hid_in, w_query, w_kv_t, w_out, meta, source_v, source,
    hid_own, hid_all, part_q, part_kv, sum_q, sum_kv, query, kv_tiles, kv_four, kv_new,
    meta_n, pool_v, leaving, kv, pick, spread,
    token_req, scores, peaks, acc, partial, received, own, gathered, send_e, recv_e,
    l_in, s_a, r_a, s_mn, r_mn, s_mig, r_mig, l_sem, s_x, r_x, s_p, r_p,
    s_b, r_b, s_bk, r_bk, s_k1, r_k1, s_k3, r_k3, s_c2, r_c2, s_k2, r_k2, s_c3, r_c3,
    s_d, r_d, s_g, r_g, s_e, r_e,
):
    w = lax.axis_index("wide")
    n = lax.axis_index("narrow")
    z = w // NY
    y = w % NY
    x = n // 2
    c = n % 2
    other = 2 * x + (1 - c)
    rows = WIDE * STEPS
    loads = []
    for i, (origin, target) in enumerate(
        (
            (moves, small.at[0]),
            (page_req, small.at[1]),
            (page_idx, small.at[2]),
            (lengths, small_len.at[0]),
            (accepted, small_len.at[1]),
            (hidden, hid_in),
            (pool, pool_v),
            (w_query_in, w_query),
            (w_kv_in, w_kv_t),
            (w_out_in, w_out),
        )
    ):
        loads.append(pltpu.make_async_copy(origin, target, l_in.at[i]))
        loads[-1].start()
    barrier = pltpu.get_barrier_semaphore()
    greet(w, n, barrier)
    for load in loads[0:6]:
        load.wait()
    hid_own[...] = jnp.zeros_like(hid_own)
    hid_own[0:STEPS, :] = hid_in[...]
    sub64 = lax.broadcasted_iota(I32, (POOL, POOL), 0).astype(F32)
    lane64 = lax.broadcasted_iota(I32, (POOL, POOL), 1).astype(F32)
    diagonal = sub64 == lane64

    def as_column(line):
        return jnp.sum(jnp.where(diagonal, line, 0.0), axis=1, keepdims=True)

    leave = small[0].astype(F32)
    leave_column = as_column(leave)
    earlier = (leave_column == leave) & (lane64 < sub64)
    rank = jnp.sum(earlier.astype(F32), axis=1, keepdims=True)
    taken = leave_column * 2.0 + rank == lane64
    req_line = small[1].astype(F32)
    idx_line = small[2].astype(F32)

    def reorder(line):
        return jnp.sum(jnp.where(taken, as_column(line), 0.0), axis=0, keepdims=True)

    source_row = jnp.sum(jnp.where(taken, sub64, 0.0), axis=0, keepdims=True).astype(I32)
    source_v[...] = jnp.zeros_like(source_v)
    source_v[0:1, 0:POOL] = source_row
    sub32 = lax.broadcasted_iota(I32, (WIDE, WIDE), 0)
    lane32 = lax.broadcasted_iota(I32, (WIDE, WIDE), 1)
    len_column = jnp.sum(
        jnp.where(sub32 == lane32, small_len[0].astype(F32), 0.0), axis=1, keepdims=True
    )
    owner_is = lax.broadcasted_iota(I32, (WIDE, POOL), 0).astype(F32) == req_line
    length_of = jnp.sum(jnp.where(owner_is, len_column, 0.0), axis=0, keepdims=True)
    seen_line = jnp.clip(length_of - idx_line * PAGE, 0.0, float(PAGE))
    seen_line = jnp.where(req_line >= 0.0, seen_line, 0.0)
    meta[...] = jnp.zeros_like(meta)
    idx_high = jnp.floor(idx_line * (1.0 / 16.0))
    hid_own[5:6, 0:POOL] = reorder(req_line).astype(BF16)
    hid_own[6:7, 0:POOL] = reorder(idx_high).astype(BF16)
    hid_own[7:8, 0:POOL] = reorder(idx_line - idx_high * 16.0).astype(BF16)
    meta[1:2, 0:POOL] = req_line.astype(I32)
    meta[1:2, POOL : 2 * POOL] = seen_line.astype(I32)
    lane_w = lax.broadcasted_iota(I32, (1, WIDE), 1)
    accepted_here = jnp.sum(
        jnp.where(lane_w == w, small_len[1].astype(F32), 0.0), axis=1, keepdims=True
    )
    to_scalar = pltpu.make_async_copy(source_v, source, l_in.at[10])
    to_scalar.start()
    hid_all[pl.ds(w, 1)] = hid_own[...][None]
    meta_n[pl.ds(n, 1)] = meta[...][None]
    pl.semaphore_wait(barrier, WIDE + NARROW - 2)

    def block_of(part, head):
        return pl.ds(pl.multiple_of(KVH * HD * part + HD * head, HD), HD)

    def exchange(dx, part):
        tx = (x + dx) % 4
        remote(
            pool.at[:, :, block_of(part, tx)],
            kv.at[n, part],
            s_x,
            r_x.at[dx - 1, part],
            (w, 2 * tx + c),
        ).start()

    for dx, part in EARLY:
        exchange(dx, part)

    def send_hidden(k, _):
        remote(hid_own, hid_all.at[w], s_a, r_a, ((w + k) % WIDE, n)).start()
        return 0

    lax.fori_loop(1, WIDE, send_hidden, 0)

    def send_meta_narrow(k, _):
        remote(meta, meta_n.at[n], s_mn, r_mn, (w, (n + k) % NARROW)).start()
        return 0

    lax.fori_loop(1, NARROW, send_meta_narrow, 0)

    for part in range(2):
        mine_here = pool.at[:, :, block_of(part, x)]
        remote(mine_here, kv.at[n, part], s_p, r_p.at[0, part], (w, other)).start()
    row = lax.broadcasted_iota(I32, (rows, WIDE * 8), 0).astype(F32)
    col = lax.broadcasted_iota(I32, (rows, WIDE * 8), 1).astype(F32)
    req_of_row = jnp.floor((row + 0.5) * 0.2)
    pick[...] = (col == req_of_row * 3.0 + row).astype(F32).astype(BF16)
    slot = lax.broadcasted_iota(I32, (WIDE * 8, rows), 0)
    req_of_slot = (slot >> 3).astype(F32)
    place = (slot & 7).astype(F32)
    origin = lax.broadcasted_iota(I32, (WIDE * 8, rows), 1).astype(F32)
    req_of_origin = jnp.floor((origin + 0.5) * 0.2)
    step_of_origin = origin - req_of_origin * 5.0
    same = req_of_slot == req_of_origin
    spread[0] = (same & (place == step_of_origin)).astype(F32).astype(BF16)
    for k in range(3):
        spread[1 + k] = (same & (place == 5.0 + k)).astype(F32).astype(BF16)
    peaks[...] = jnp.full(peaks.shape, NEG, F32)
    acc[...] = jnp.zeros_like(acc)

    to_scalar.wait()
    loads[6].wait()

    def take_page(j, _):
        leaving[j] = pool_v[jnp.clip(source[0, j], 0, POOL - 1)]
        for part in range(2):
            kv[n, part, j] = pool_v[j, :, block_of(part, x)]
        return 0

    lax.fori_loop(0, POOL, take_page, 0)
    stay = pltpu.make_async_copy(
        leaving.at[pl.ds(2 * w, 2)], moved_out.at[pl.ds(2 * w, 2)], l_sem.at[3]
    )
    stay.start()

    def send_pages(first, last):
        def send_pair(i, _):
            for k in (i, WIDE - i):
                peer = (w + k) % WIDE
                remote(
                    leaving.at[pl.ds(2 * peer, 2)],
                    moved_out.at[pl.ds(2 * w, 2)],
                    s_mig,
                    r_mig,
                    (peer, n),
                ).start()
            return 0

        lax.fori_loop(first, min(last, 16), send_pair, 0)
        if first <= 16 < last:
            peer = (w + 16) % WIDE
            remote(
                leaving.at[pl.ds(2 * peer, 2)],
                moved_out.at[pl.ds(2 * w, 2)],
                s_mig,
                r_mig,
                (peer, n),
            ).start()

    send_pages(1, CUT0)
    others = hid_all.at[pl.ds(0, WIDE - 1)]
    all_hidden = remote(others, others, s_a, r_a, (w, n))
    all_hidden.wait_recv()
    padded = hid_all[...].reshape(WIDE * 8, hid_all.shape[2])
    loads[7].wait()
    loads[8].wait()
    packed = jnp.dot(pick[...], padded, preferred_element_type=F32).astype(BF16)
    part_q[...] = jnp.dot(packed, w_query[...], preferred_element_type=F32).astype(BF16)
    to_hub_q = remote(part_q, sum_q.at[n], s_b, r_b, (w, z))
    to_hub_kv = remote(part_kv, sum_kv.at[n], s_bk, r_bk, (w, z))

    @pl.when(n != z)
    def _():
        to_hub_q.start()

    new_kv = lax.dot_general(
        padded, w_kv_t[...], (((1,), (1,)), ((), ())), preferred_element_type=F32
    )
    for j in range(4):
        part_kv[:, 32 * j : 32 * j + 32] = new_kv[64 * j : 64 * j + 64].astype(BF16)

    @pl.when(n != z)
    def _():
        to_hub_kv.start()

    for dx, part in LATE:
        exchange(dx, part)
    send_pages(CUT0, CUT1)
    mine = query.at[y]
    seven_q = sum_q.at[pl.ds(0, 7)]
    seven_kv = sum_kv.at[pl.ds(0, 7)]

    @pl.when(n == z)
    def _():
        sum_q[pl.ds(n, 1)] = part_q[...][None]
        remote(seven_q, seven_q, s_b, r_b, (w, n)).wait_recv()
        query[pl.ds(y, 1)] = jnp.sum(sum_q[...].astype(F32), axis=0).astype(BF16)[None]

        def send_query(k, _):
            peer = ((z + k) % NZ) * NY + y
            remote(mine, mine, s_c2, r_c2, (peer, n)).start()
            return 0

        lax.fori_loop(1, NZ, send_query, 0)

    @pl.when(n != z)
    def _():
        remote(mine, mine, s_c2, r_c2, (w, n)).wait_recv()

    for dy in (1, 3, 2):
        remote(mine, mine, s_c3, r_c3, (z * NY + (y + dy) % NY, n)).start()

    @pl.when(n == z)
    def _():
        sum_kv[pl.ds(n, 1)] = part_kv[...][None]
        remote(seven_kv, seven_kv, s_bk, r_bk, (w, n)).wait_recv()
        kv_tiles[...] = jnp.sum(sum_kv[...].astype(F32), axis=0).astype(BF16).reshape(8, 8, HD)
        kv_four[pl.ds(y, 1)] = kv_tiles[...][None]

        def send_tile(k, _):
            peer = ((z + k) % NZ) * NY + y
            remote(kv_tiles, kv_four.at[y], s_k1, r_k1, (peer, n)).start()
            return 0

        lax.fori_loop(1, NZ, send_tile, 0)

    send_pages(CUT1, CUT2)

    def relay(dx, part):
        here = kv.at[2 * ((x + 4 - dx) % 4) + c, part]
        remote(here, here, s_x, r_x.at[dx - 1, part], (w, n)).wait_recv()
        remote(here, here, s_p, r_p.at[dx, part], (w, other)).start()

    for dx, part in EARLY:
        relay(dx, part)
    mine_kv = kv_four.at[y]

    @pl.when(n != z)
    def _():
        remote(mine_kv, mine_kv, s_k1, r_k1, (w, n)).wait_recv()

    for dy in (1, 3, 2):
        remote(mine_kv, mine_kv, s_k3, r_k3, (z * NY + (y + dy) % NY, n)).start()
    narrow_tiles = meta_n.at[pl.ds(0, NARROW - 1)]
    remote(narrow_tiles, narrow_tiles, s_mn, r_mn, (w, n)).wait()
    page_meta = meta_n[:, 1, :].astype(F32).astype(BF16)
    page = lax.broadcasted_iota(I32, (2 * POOL, POOL * PAGE), 0)
    page_of = lax.broadcasted_iota(I32, (2 * POOL, POOL * PAGE), 1) >> 4
    spread_req = (page == page_of).astype(F32).astype(BF16)
    spread_seen = (page - POOL == page_of).astype(F32).astype(BF16)
    owner = jnp.dot(page_meta, spread_req, preferred_element_type=F32)
    seen = jnp.dot(page_meta, spread_seen, preferred_element_type=F32)
    within = (lax.broadcasted_iota(I32, (NARROW, POOL * PAGE), 1) & 15).astype(F32)
    owner = jnp.where(within < seen, owner, -1.0)
    width = CHUNK * PAGE
    per = POOL // CHUNK
    for s in range(NARROW):
        for i in range(per):
            token_req[per * s + i] = jnp.broadcast_to(
                owner[s : s + 1, width * i : width * i + width], (8, width)
            )
    all_row = lax.broadcasted_iota(I32, (rows, 1), 0).astype(F32)
    row_req = jnp.floor((all_row + 0.5) * 0.2)
    row_req = jnp.concatenate([row_req] * 4, axis=0)
    three = query.at[pl.ds(0, 3)]
    spread_query = remote(three, three, s_c3, r_c3, (w, n))
    spread_query.wait_recv()

    for g, dx in enumerate(ORDER):
        from_other = kv.at[2 * ((x + 4 - dx) % 4) + (1 - c), 0]
        remote(from_other, from_other, s_p, r_p.at[dx, 0], (w, n)).wait_recv()

        def score(j, _, g=g, dx=dx):
            s = 2 * ((x + 4 - dx) % 4) + j // per
            i = j % per
            keys = kv[s, 0, pl.ds(i * CHUNK, CHUNK)].reshape(width, HD)
            raw = lax.dot_general(
                query[...].reshape(4 * rows, HD),
                keys,
                (((1,), (1,)), ((), ())),
                preferred_element_type=F32,
            )
            owners = token_req[per * s + i][0:1, :]
            raw = jnp.where(row_req == owners, raw, NEG)
            scores[2 * per * g + j] = raw
            top = raw[:, 0:HD]
            for t in range(1, width // HD):
                top = jnp.maximum(top, raw[:, HD * t : HD * t + HD])
            peaks[...] = jnp.maximum(peaks[...], top)
            return 0

        lax.fori_loop(0, 2 * per, score, 0)

    for dx, part in LATE:
        relay(dx, part)
    peak = jnp.max(peaks[...], axis=1, keepdims=True)
    ones = jnp.ones((width, HD), BF16)
    for g, dx in enumerate(ORDER):
        from_other = kv.at[2 * ((x + 4 - dx) % 4) + (1 - c), 1]
        remote(from_other, from_other, s_p, r_p.at[dx, 1], (w, n)).wait_recv()

        def weigh(j, _, g=g, dx=dx):
            s = 2 * ((x + 4 - dx) % 4) + j // per
            i = j % per
            values = kv[s, 1, pl.ds(i * CHUNK, CHUNK)].reshape(width, HD)
            weights = jnp.exp2(
                (scores[2 * per * g + j] - peak) * (SCALE * LOG2E)
            ).astype(BF16)
            acc[...] += jnp.dot(
                weights, jnp.concatenate([values, ones], axis=1), preferred_element_type=F32
            )
            return 0

        lax.fori_loop(0, 2 * per, weigh, 0)

    group = (lax.broadcasted_iota(I32, (rows, HD), 1) >> 3).astype(F32)
    srow = lax.broadcasted_iota(I32, (rows, HD), 0).astype(F32)
    step_of = srow - jnp.floor((srow + 0.5) * 0.2) * 5.0
    for h in range(4):
        here = slice(rows * h, rows * h + rows)
        terms = payload_stats(peak[here] * SCALE, acc[here, HD:], group, step_of)
        laid = jnp.dot(spread[0], acc[here, 0:HD].astype(BF16), preferred_element_type=F32)
        for k in range(3):
            laid += jnp.dot(spread[1 + k], terms[k], preferred_element_type=F32)
        partial[:, h] = laid.astype(BF16).reshape(WIDE, 8, HD)

    def send_partial(k, _):
        peer = (w + k) % WIDE
        remote(partial.at[peer], received.at[w], s_d, r_d, (peer, n)).start()
        return 0

    lax.fori_loop(1, WIDE, send_partial, 0)
    received[pl.ds(w, 1)] = partial[pl.ds(w, 1)]
    send_pages(CUT2, CUT3)

    lane = lax.broadcasted_iota(I32, (8, HD), 1)
    three_kv = kv_four.at[pl.ds(0, 3)]
    remote(three_kv, three_kv, s_k3, r_k3, (w, n)).wait()
    merged = jnp.zeros((8, HD), F32)
    for t in range(4):
        turned = pltpu.roll(kv_four[t, w % 8].astype(F32), (t + 4 - w // 8) % 4 * 32, 1)
        merged = merged + jnp.where((lane >= 32 * t) & (lane < 32 * t + 32), turned, 0.0)
    kv_new[pl.ds(n, 1)] = merged.astype(BF16)[None]

    def send_new(k, _):
        remote(kv_new.at[n], kv_new.at[n], s_k2, r_k2, (w, (n + k) % NARROW)).start()
        return 0

    lax.fori_loop(1, NARROW, send_new, 0)
    meta_lane = lax.broadcasted_iota(I32, (WIDE, HD), 1)
    slot_source = lax.broadcasted_iota(I32, (WIDE, POOL), 0)
    slot_lane = lax.broadcasted_iota(I32, (WIDE, POOL), 1)

    def arrived(line):
        values = hid_all[:, line : line + 1, 0:HD].astype(F32).reshape(WIDE, HD)
        result = jnp.zeros((1, POOL), F32)
        for k in range(2):
            column = jnp.sum(
                jnp.where(meta_lane == 2 * w + k, values, 0.0), axis=1, keepdims=True
            )
            result = result + jnp.sum(
                jnp.where(slot_lane == 2 * slot_source + k, column, 0.0), axis=0, keepdims=True
            )
        return result

    moved_req[...] = arrived(5).astype(I32)
    moved_idx[...] = (arrived(6) * 16.0 + arrived(7)).astype(I32)
    seven_new = kv_new.at[pl.ds(0, 7)]
    remote(seven_new, seven_new, s_k2, r_k2, (w, n)).wait()
    step = lax.broadcasted_iota(I32, (STEPS, HD), 0).astype(F32)
    for b in range(8):
        entries[0, :, HD * b : HD * b + HD] = jnp.where(
            step < accepted_here, kv_new[b][0:STEPS, :].astype(F32), 0.0
        ).astype(BF16)

    first_row = lax.broadcasted_iota(I32, (32, rows), 0)
    from_row = lax.broadcasted_iota(I32, (32, rows), 1)
    ours = (from_row == 5 * w + (first_row & 7)) & ((first_row & 7) < STEPS)
    ours = ours.astype(F32).astype(BF16)
    k_new = kv_new[x]
    v_new = kv_new[KVH + x]
    sub = lax.broadcasted_iota(I32, (8, HD), 0)
    lane_group = lane >> 3
    fresh_row = lax.broadcasted_iota(I32, (8, 8), 0)
    fresh_key = lax.broadcasted_iota(I32, (8, 8), 1)
    known = fresh_key <= fresh_row
    for h in range(4):
        q_new = jnp.dot(ours[0:8], query[h], preferred_element_type=F32).astype(BF16)
        fresh = lax.dot_general(
            q_new, k_new, (((1,), (1,)), ((), ())), preferred_element_type=F32
        ) * SCALE
        fresh = jnp.where(known, fresh, NEG)
        fresh_peak = jnp.max(fresh, axis=1, keepdims=True)
        fresh_weight = jnp.where(known, jnp.exp(fresh - fresh_peak), 0.0)
        fresh_total = jnp.sum(fresh_weight, axis=1, keepdims=True)
        fresh_sum = jnp.dot(fresh_weight.astype(BF16), v_new, preferred_element_type=F32)
        stat = jnp.where(
            lane_group == sub,
            fresh_peak,
            jnp.where(lane_group - 8 == sub, fresh_total, 0.0),
        )
        line = jnp.sum(jnp.where(sub < STEPS, stat, 0.0), axis=0, keepdims=True)
        first = line.astype(BF16).astype(F32)
        second = (line - first).astype(BF16).astype(F32)
        third = line - first - second
        tile = jnp.where(
            sub < STEPS,
            fresh_sum,
            jnp.where(sub == 5, first, jnp.where(sub == 6, second, third)),
        )
        received[WIDE, h] = tile.astype(BF16)

    others = received.at[pl.ds(0, WIDE - 1)]
    all_partial = remote(others, others, s_d, r_d, (w, n))
    all_partial.wait_recv()
    sub3 = lax.broadcasted_iota(I32, (1, 8, HD), 1)
    group3 = lax.broadcasted_iota(I32, (1, 8, HD), 2) >> 3
    for h in range(4):
        tiles = received[:, h].astype(F32)
        line = (tiles[:, 7:8] + tiles[:, 6:7]) + tiles[:, 5:6]
        high = jnp.max(jnp.where(group3 == sub3, line, -3e38), axis=2, keepdims=True)
        total = jnp.max(jnp.where(group3 - 8 == sub3, line, 0.0), axis=2, keepdims=True)
        top = jnp.max(high, axis=0, keepdims=True)
        factor = jnp.exp(high - top)
        total = jnp.sum(factor * total, axis=0)
        sums = jnp.sum(factor * tiles, axis=0)
        own[:, HD * h : HD * h + HD] = jnp.where(
            sub < STEPS, sums / jnp.where(sub < STEPS, total, 1.0), 0.0
        ).astype(BF16)
    gathered[pl.ds(w, 1)] = own[...][None]

    def send_own(k, _):
        remote(own, gathered.at[w], s_g, r_g, ((w + k) % WIDE, n)).start()
        return 0

    lax.fori_loop(1, WIDE, send_own, 0)
    send_pages(CUT3, 17)
    others = gathered.at[pl.ds(0, WIDE - 1)]
    all_rows = remote(others, others, s_g, r_g, (w, n))
    all_rows.wait_recv()
    loads[9].wait()
    attn = gathered[...].reshape(WIDE * 8, gathered.shape[2])
    product = jnp.dot(attn, w_out[...], preferred_element_type=F32)
    send_e[...] = product.astype(BF16).reshape(NARROW, 32, HD)
    recv_e[pl.ds(n, 1)] = send_e[pl.ds(n, 1)]

    def send_product(k, _):
        peer = (n + k) % NARROW
        remote(send_e.at[peer], recv_e.at[n], s_e, r_e, (w, peer)).start()
        return 0

    lax.fori_loop(1, NARROW, send_product, 0)
    others = recv_e.at[pl.ds(0, NARROW - 1)]
    all_products = remote(others, others, s_e, r_e, (w, n))
    all_products.wait_recv()
    result = jnp.sum(recv_e[...].astype(F32), axis=0)
    for j in range(4):
        attended[STEPS * j : STEPS * j + STEPS, :] = result[8 * j : 8 * j + STEPS].astype(BF16)

    all_hidden.wait_send()
    spread_query.wait_send()
    three = kv.at[pl.ds(0, 3)]
    remote(three, three, s_x, r_x.at[0, 0], (w, n)).wait_send()
    four = kv.at[pl.ds(0, 4)]
    remote(four, four, s_p, r_p.at[0, 0], (w, n)).wait_send()

    @pl.when(n != z)
    def _():
        to_hub_q.wait_send()
        to_hub_kv.wait_send()

    three_kv = kv_four.at[pl.ds(0, 3)]

    @pl.when(n == z)
    def _():
        remote(kv_four, kv_four, s_k1, r_k1, (w, n)).wait_send()
        remote(three_kv, three_kv, s_k1, r_k1, (w, n)).wait_send()
        four_q = query
        three_q = query.at[pl.ds(0, 3)]
        remote(four_q, four_q, s_c2, r_c2, (w, n)).wait_send()
        remote(three_q, three_q, s_c2, r_c2, (w, n)).wait_send()

    all_partial.wait_send()
    all_rows.wait_send()
    all_products.wait_send()
    stay.wait()
    gone = moved_out.at[pl.ds(0, POOL - 2)]
    remote(gone, gone, s_mig, r_mig, (w, n)).wait()


def deliver_kernel(*refs):
    sources, targets, (pages, sem_in, sem_out, sem_small) = refs[0:5], refs[5:10], refs[10:14]
    size = POOL // PIECES
    small = [
        pltpu.make_async_copy(sources[i], targets[i], sem_small.at[i]) for i in (0, 1, 3, 4)
    ]
    for copy in small:
        copy.start()
    parts = [pl.ds(size * i, size) for i in range(PIECES)]
    coming = [
        pltpu.make_async_copy(sources[2].at[part], pages.at[part], sem_in.at[i])
        for i, part in enumerate(parts)
    ]
    going = [
        pltpu.make_async_copy(pages.at[part], targets[2].at[part], sem_out.at[i])
        for i, part in enumerate(parts)
    ]
    for copy in coming:
        copy.start()
    for before, after in zip(coming, going):
        before.wait()
        after.start()
    for copy in going + small:
        copy.wait()


def on_device(hidden, w_query, w_keyval, w_out, pool, page_req, page_idx, lengths, moves, accepted):
    dma = pltpu.SemaphoreType.DMA
    shape = jax.ShapeDtypeStruct
    depth = hidden.shape[1]
    rows = WIDE * STEPS
    width = CHUNK * PAGE
    chunks = NARROW * POOL // CHUNK
    results = pl.pallas_call(
        whole_kernel,
        out_shape=(
            shape((4 * STEPS, HD), BF16),
            shape((1, STEPS, 1024), BF16),
            shape(pool.shape, BF16),
            shape((1, POOL), I32),
            shape((1, POOL), I32),
        ),
        in_specs=[ANY_SPEC] * 10,
        out_specs=(VMEM_SPEC, VMEM_SPEC, ANY_SPEC, VMEM_SPEC, VMEM_SPEC),
        scratch_shapes=[
            pltpu.VMEM((3, 1, POOL), I32),
            pltpu.VMEM((2, 1, WIDE), I32),
            pltpu.VMEM((STEPS, depth), BF16),
            pltpu.VMEM(w_query.shape, BF16),
            pltpu.VMEM(w_keyval.shape[::-1], BF16),
            pltpu.VMEM(w_out.shape, BF16),
            pltpu.VMEM((8, 128), I32),
            pltpu.VMEM((8, 128), I32),
            pltpu.SMEM((8, 128), I32),
            pltpu.VMEM((8, depth), BF16),
            pltpu.VMEM((WIDE, 8, depth), BF16),
            pltpu.VMEM((rows, HD), BF16),
            pltpu.VMEM((64, HD), BF16),
            pltpu.VMEM((NARROW, rows, HD), BF16),
            pltpu.VMEM((NARROW, 64, HD), BF16),
            pltpu.VMEM((4, rows, HD), BF16),
            pltpu.VMEM((8, 8, HD), BF16),
            pltpu.VMEM((4, 8, 8, HD), BF16),
            pltpu.VMEM((8, 8, HD), BF16),
            pltpu.VMEM((NARROW, 8, 128), I32),
            pltpu.VMEM(pool.shape, BF16),
            pltpu.VMEM(pool.shape, BF16),
            pltpu.VMEM((NARROW, 2, POOL, PAGE, HD), BF16),
            pltpu.VMEM((rows, WIDE * 8), BF16),
            pltpu.VMEM((4, WIDE * 8, rows), BF16),
            pltpu.VMEM((chunks, 8, width), F32),
            pltpu.VMEM((chunks, 4 * rows, width), F32),
            pltpu.VMEM((4 * rows, HD), F32),
            pltpu.VMEM((4 * rows, 2 * HD), F32),
            pltpu.VMEM((WIDE, 4, 8, HD), BF16),
            pltpu.VMEM((WIDE + 1, 4, 8, HD), BF16),
            pltpu.VMEM((8, 4 * HD), BF16),
            pltpu.VMEM((WIDE, 8, 4 * HD), BF16),
            pltpu.VMEM((NARROW, 32, HD), BF16),
            pltpu.VMEM((NARROW, 32, HD), BF16),
            dma((11,)), dma, dma, dma, dma, dma, dma,
            dma((5,)), dma, dma((3, 2)), dma, dma((4, 2)),
            dma, dma, dma, dma, dma, dma, dma, dma, dma, dma, dma, dma,
            dma, dma, dma, dma, dma, dma, dma, dma,
        ],
        compiler_params=pltpu.CompilerParams(
            collective_id=0, has_side_effects=True, vmem_limit_bytes=60 << 20
        ),
        name="verify_step",
    )(
        moves.reshape(1, POOL),
        page_req.reshape(1, POOL),
        page_idx.reshape(1, POOL),
        lengths.reshape(1, WIDE),
        accepted.reshape(1, WIDE),
        hidden,
        w_query,
        w_keyval.T,
        w_out,
        pool,
    )
    attended, entries, moved, moved_req, moved_idx = pl.pallas_call(
        deliver_kernel,
        out_shape=[shape(r.shape, r.dtype) for r in results],
        in_specs=[ANY_SPEC] * 5,
        out_specs=[ANY_SPEC] * 5,
        scratch_shapes=[
            pltpu.VMEM(pool.shape, BF16),
            dma((PIECES,)),
            dma((PIECES,)),
            dma((5,)),
        ],
        name="deliver",
    )(*results)
    return attended, entries, moved, moved_req.reshape(POOL), moved_idx.reshape(POOL)


def solution(mesh):
    in_specs = (
        P("wide", "narrow"),
        P("narrow", "wide"),
        P("narrow", "wide"),
        P("narrow", "wide"),
        P(("wide", "narrow"), None, None),
        P(("wide", "narrow")),
        P(("wide", "narrow")),
        P(),
        P(("wide", "narrow"), None),
        P(),
    )
    out_specs = (
        P("narrow", "wide"),
        P("wide", None, None),
        P(("wide", "narrow"), None, None),
        P(("wide", "narrow")),
        P(("wide", "narrow")),
    )
    return jax.shard_map(
        on_device, mesh=mesh, in_specs=in_specs, out_specs=out_specs, check_vma=False
    )
```
